128 devices in a mesh: cube: 2 (over core), half: 2 (over z_hi), grid: 32 (over y, x, z_lo).
Axes of the slice: x: 4, y: 4, z: 4 (z_hi: 2, z_lo: 2; z = z_hi * 2 + z_lo), core: 2. Of those that a mesh axis runs over, the one named last changes fastest.
Arguments:
- child_blocks: float32 [4, 8192, 8192], P(('cube', 'half'), None, 'grid'), parts along dimension 0, as said below
- child_map: int32 [4, 64], P('cube'), parts along dimension 0, may hold values from 0 to 95, as said below
- block_at: int32 [192], P('cube'), parts along dimension 0, may hold values from 0 to 95, as said below
- pattern: int32 [176, 8], P('cube'), parts along dimension 0, may hold values 0 or 1
Outputs:
- factored: float32 [24576, 12288], P(('cube', 'half'), 'grid'), parts along dimension 0
The draws below stay inside these ranges and needn't reach their ends.
There are 2 independent parts, one for each index of `cube`. The reference program is written for one: setup_inputs(seed, part) draws one part's arguments, and reference() takes and returns one part's arrays. A program takes and returns all parts, laid end to end along the dimension named above; each array names one. Nothing has to cross between parts.
Inputs may be any that keep to these rules, and one draw needn't show every extreme that they name: block_at is a permutation of the 96 front blocks. Each row of child_map holds 64 distinct front blocks. For child c and child block b, the storage index s with block_at[s] = child_map[c, b] satisfies s // 3 == b // 2. Every pivot block, front blocks 0 to 7, appears in both rows. Each child_blocks[c] is symmetric.
All inputs are finite; a program needn't handle non-finite values.
Results may differ from the reference program's by a relative error of at most 0.0001.
Values sent between devices are 32-bit elements; how exact they have to be, the bound alone decides.
A program may use at most 192 MiB of HBM per device.

```python
import math
import jax
import jax.numpy as jnp
from jax import lax

F = 12288
CU = 8192
BS = 128
PIV = 512
PANELS = 2
NB = 96
CB = 64
PB = 8
OWN = 3
HELD = 2


def layout_tables(key):
    grids = NB // OWN
    base = jax.random.fold_in(key, 7001)
    covers = []
    for child_no in range(2):
        scores = jax.random.randint(jax.random.fold_in(base, child_no), (grids, OWN), 0, 1 << 20)
        scores = scores * OWN + jnp.arange(OWN, dtype=jnp.int32)[None, :]
        ranked = jnp.argsort(scores, axis=1).astype(jnp.int32)
        chosen = ranked[:, :HELD] + (jnp.arange(grids, dtype=jnp.int32) * OWN)[:, None]
        covers.append(chosen.reshape(CB))
    slots = jnp.arange(NB, dtype=jnp.int32)
    counted = jnp.zeros((NB,), jnp.int32)
    for child_no in range(2):
        counted = counted + jnp.sum((covers[child_no][:, None] == slots[None, :]).astype(jnp.int32), axis=0)
    scores = jax.random.randint(jax.random.fold_in(base, 5), (NB,), 0, 1 << 20) * NB + slots
    scores = jnp.where(counted == 2, scores, scores + (1 << 20) * NB)
    ranked = jnp.argsort(scores).astype(jnp.int32)
    block_at = jnp.argsort(ranked).astype(jnp.int32)
    child_map = jnp.stack([block_at[covers[0]], block_at[covers[1]]])
    return (block_at, child_map)


def draw_block_at(key, part):
    return layout_tables(key)[0]


def draw_child_map(key, part):
    return layout_tables(key)[1]


def draw_child_blocks(key, part):
    spread = 1.28 / math.sqrt(PANELS * PIV)
    mats = []
    for child_no in range(2):
        first_key, second_key = jax.random.split(jax.random.fold_in(key, 300 + child_no))
        noise = jax.random.normal(first_key, (CU, CU), jnp.float32)
        symmetric = (noise + noise.T) * (spread / math.sqrt(2.0))
        diagonal = jax.random.uniform(second_key, (CU,), jnp.float32, 2.5, 5.0)
        mats.append(symmetric + jnp.diag(diagonal))
    return jnp.stack(mats)


def with_ends(drawn, rng, low, largest):
    place = [jax.random.randint(jax.random.fold_in(rng, axis), (), 0, length) for axis, length in enumerate(drawn.shape)]
    widest = drawn.shape.index(max(drawn.shape))
    beside = place[:widest] + [(place[widest] + 1) % drawn.shape[widest]] + place[widest + 1:]
    return drawn.at[tuple(place)].set(low).at[tuple(beside)].set(largest)


def setup_inputs(seed: int = 0, part: int = 0) -> dict:
    arg_keys = jax.random.split(jax.random.key(seed), 5)
    part_keys = jax.random.split(jax.random.fold_in(arg_keys[4], part), 5)
    return {
        "child_blocks": draw_child_blocks(jax.random.fold_in(jax.random.fold_in(arg_keys[4], part), 71), part),
        "child_map": draw_child_map(jax.random.fold_in(jax.random.fold_in(arg_keys[4], part), 71), part),
        "block_at": draw_block_at(jax.random.fold_in(jax.random.fold_in(arg_keys[4], part), 71), part),
        "pattern": with_ends((jax.random.randint(part_keys[3], (NB - PB, PB), 0, 4) < 3).astype(jnp.int32), jax.random.fold_in(part_keys[3], 1), 0, 1),
    }


def block_mask(pattern):
    lower_part = jnp.concatenate([jnp.ones((PB, PB), jnp.float32), pattern.astype(jnp.float32)], axis=0)
    mask_table = jnp.ones((NB, NB), jnp.float32)
    mask_table = mask_table.at[:, :PB].set(lower_part)
    mask_table = mask_table.at[:PB, :].set(lower_part.T)
    return mask_table

def reference(child_blocks, child_map, block_at, pattern):
    assembled = jnp.zeros((NB, NB, BS, BS), jnp.float32)
    for child_no in range(2):
        pieces = child_blocks[child_no].reshape(CB, BS, CB, BS).transpose(0, 2, 1, 3)
        targets = child_map[child_no]
        assembled = assembled.at[targets[:, None], targets[None, :]].add(pieces)
    assembled = assembled * block_mask(pattern)[:, :, None, None]
    matrix = assembled.transpose(0, 2, 1, 3).reshape(F, F)
    identity = jnp.eye(PIV, dtype=jnp.float32)
    for panel in range(PANELS):
        start_col = panel * PIV
        end_col = start_col + PIV
        columns = matrix[:, start_col:end_col]
        factor = jnp.linalg.cholesky(columns[start_col:end_col])
        inverse = lax.linalg.triangular_solve(factor, identity, left_side=True, lower=True)
        beneath = jnp.dot(columns[end_col:], inverse.T, precision=lax.Precision.HIGHEST)
        update = jnp.dot(beneath, beneath.T, precision=lax.Precision.HIGHEST)
        matrix = matrix.at[end_col:, end_col:].add(-update)
        new_cols = jnp.concatenate([jnp.zeros((start_col, PIV), jnp.float32), jnp.tril(factor), beneath], axis=0)
        matrix = matrix.at[:, start_col:end_col].set(new_cols)
        matrix = matrix.at[start_col:end_col, end_col:].set(0.0)
    pieces = matrix.reshape(NB, BS, NB, BS)
    pieces = pieces[block_at][:, :, block_at]
    return pieces.reshape(F, F)
```

```python
import jax
import jax.numpy as jnp
from jax import lax
from jax.experimental import pallas as pl
from jax.experimental.pallas import tpu as pltpu
from jax.sharding import PartitionSpec as P

BS = 128
PB = 8
PV = PB * BS
OWN = 3
HELD = 2
CW = HELD * BS
FW = OWN * BS
GRID = 32
PEERS = 2 * GRID
CB = 64
NB = 96
TR = FW // 2
TK = PV // 2
TRI = (PB + 1) * BS
MESH = pl.DeviceIdType.MESH
HI = lax.Precision.HIGHEST
MIB = 1 << 20


def contract(a, b, dims):
    return lax.dot_general(
        a, b, (dims, ((), ())), precision=HI, preferred_element_type=jnp.float32
    )


SECOND, COLUMN, KEEP, PLAIN, UNIT, COEFS = 0, 16, 28, 52, 55, 80


def pick_rows(map_ref, at_ref, pat_ref, child_ref, x_ref, xp_ref, from_ref, coef_ref, found, sems):
    half = lax.axis_index("half")
    grid = lax.axis_index("grid")

    def scan(b, carry):
        for c in range(2):
            f = map_ref[c, b]

            @pl.when(f < PB)
            def _():
                found[c * PB + f] = b

        return carry

    lax.fori_loop(0, CB, scan, 0)

    def copy(p):
        b = found[half * PB + p]
        return pltpu.make_async_copy(
            child_ref.at[0, pl.ds(pl.multiple_of(b * BS, BS), BS), :],
            x_ref.at[pl.ds(p * BS, BS), :],
            sems.at[p],
        )

    for p in range(PB):
        copy(p).start()
    for c in range(2):
        for p in range(PB):
            b = found[c * PB + p]
            from_ref[c * PB + p] = c * GRID + (b >> 1)
            coef_ref[SECOND + c * PB + p] = (b & 1).astype(jnp.float32)
    for j in range(OWN):
        q = at_ref[grid * OWN + j]
        for t in range(HELD):
            for side in range(2):
                hit = map_ref[jnp.where(side == 0, half, 1 - half), grid * HELD + t] == q
                coef_ref[COLUMN + 4 * j + 2 * t + side] = jnp.where(hit, 1.0, 0.0)
        for p in range(PB):
            keep = jnp.where(q < PB, 1, pat_ref[jnp.maximum(q - PB, 0), p])
            coef_ref[KEEP + PB * j + p] = keep.astype(jnp.float32)
            coef_ref[UNIT + PB * j + p] = jnp.where(q == p, -1.0, 0.0)
        coef_ref[PLAIN + j] = jnp.where(q < PB, 0.0, 1.0)
    for p in range(PB):
        copy(p).wait()
    for d in range(PEERS):
        xp_ref[d, 0:8, :] = x_ref[8 * d : 8 * d + 8, :]
        xp_ref[d, 8:16, :] = x_ref[PV - 8 * d - 8 : PV - 8 * d, :]


def factor_block(dy, out):
    sub = lax.broadcasted_iota(jnp.int32, (8, BS), 0)
    lane = lax.broadcasted_iota(jnp.int32, (8, BS), 1)
    for q in range(BS // 8):
        j0 = 8 * q
        ra = dy[j0 : j0 + 8, 0:BS]
        ry = dy[j0 : j0 + 8, BS : 2 * BS]
        cols = [jnp.broadcast_to(ra[:, j0 + r : j0 + r + 1], (8, BS)) for r in range(8)]
        scale = jnp.ones((8, BS), jnp.float32)
        for r in range(8):
            inv = lax.rsqrt(cols[r][r : r + 1, :])
            scale = jnp.where(sub == r, inv, scale)
            if r == 7:
                break
            part = jnp.where(sub > r, cols[r] * (inv * inv), 0.0)
            for c in range(r + 1, 8):
                cols[c] = cols[c] - part * cols[c][r : r + 1, :]
            ra = ra - part * ra[r : r + 1, :]
            ry = ry - part * ry[r : r + 1, :]
        ra = jnp.where(lane >= sub + j0, ra * scale, 0.0)
        ry = ry * scale
        both = jnp.concatenate([ra, ry], axis=1)
        out[j0 : j0 + 8, :] = both
        if q < BS // 8 - 1:
            step = contract(ra, both, ((0,), (0,)))
            dy[j0 + 8 :, :] = dy[j0 + 8 :, :] - step[j0 + 8 :, :]


def exchange(
    from_ref, coef_ref, x_ref, xp_ref, child_ref,
    gall, recvc, w_ref, l_ref,
    xo, ra, pk, rp, mc, gt, pm, dinv, dy, uy, tcol,
    ss, rs, psend, precv, loc,
):
    cube = lax.axis_index("cube")
    half = lax.axis_index("half")
    grid = lax.axis_index("grid")
    me = half * GRID + grid
    y, x, zl = grid >> 3, (grid >> 1) & 3, grid & 1
    r = (y - 2 * half) & 3

    def dev(yy, xx, zz):
        return (cube, half, (yy & 3) * 8 + (xx & 3) * 2 + zz)

    partner = (cube, 1 - half, grid)

    def remote(k, src, dst, to):
        return pltpu.make_async_remote_copy(
            src_ref=src, dst_ref=dst, send_sem=ss.at[k], recv_sem=rs.at[k],
            device_id=to, device_id_type=MESH,
        )

    XS, S0, S1, ZX = 40, 41, 42, 43

    swap = remote(XS, x_ref, xo, partner)
    swap.start()

    def spread_rows(i, carry):
        to = (me + i) & (PEERS - 1)
        pltpu.make_async_remote_copy(
            src_ref=xp_ref.at[to], dst_ref=ra.at[me], send_sem=psend.at[0], recv_sem=precv.at[0],
            device_id=(cube, to >> 5, to & (GRID - 1)), device_id_type=MESH,
        ).start()
        return carry

    lax.fori_loop(1, PEERS, spread_rows, 0)
    ra[me] = xp_ref[me]
    rows_in = pltpu.make_async_remote_copy(
        src_ref=xp_ref.at[pl.ds(0, PEERS - 1)], dst_ref=ra.at[pl.ds(0, PEERS - 1)],
        send_sem=psend.at[0], recv_sem=precv.at[0], device_id=partner, device_id_type=MESH,
    )
    l_ref[...] = jnp.zeros_like(l_ref)
    rows_in.wait_recv()

    first = (me >> 4) + 1
    for k in range(PB + 1):
        low = k < first
        p = jnp.where(low, k, k - first)
        total = jnp.zeros((8, BS), jnp.float32)
        for c in range(2):
            came = ra[from_ref[c * PB + p]]
            second = coef_ref[SECOND + c * PB + p]
            came = jnp.where(low, came[0:8, :], came[8:16, :])
            total = total + came[:, 0:BS] * (1.0 - second) + came[:, BS:] * second
        pk[:, k * BS : (k + 1) * BS] = total

    def spread_pivot(i, carry):
        to = (me + i) & (PEERS - 1)
        pltpu.make_async_remote_copy(
            src_ref=pk, dst_ref=rp.at[me], send_sem=psend.at[1], recv_sem=precv.at[1],
            device_id=(cube, to >> 5, to & (GRID - 1)), device_id_type=MESH,
        ).start()
        return carry

    lax.fori_loop(1, PEERS, spread_pivot, 0)
    rp[me] = pk[...]
    pivot_in = pltpu.make_async_remote_copy(
        src_ref=rp.at[pl.ds(0, PEERS - 1)], dst_ref=rp.at[pl.ds(0, PEERS - 1)],
        send_sem=psend.at[1], recv_sem=precv.at[1], device_id=partner, device_id_type=MESH,
    )

    swap.wait_recv()
    for j in range(OWN):

        def assemble(p, carry, j=j):
            rows = pl.ds(pl.multiple_of(p * BS, BS), BS)
            keep = coef_ref[KEEP + PB * j + p]
            total = jnp.zeros((BS, BS), jnp.float32)
            for t in range(HELD):
                cols = slice(t * BS, (t + 1) * BS)
                total += x_ref[rows, cols] * coef_ref[COLUMN + 4 * j + 2 * t]
                total += xo[rows, cols] * coef_ref[COLUMN + 4 * j + 2 * t + 1]
            mc[rows, j * BS : (j + 1) * BS] = total * keep
            return carry

        lax.fori_loop(0, PB, assemble, 0)

    source = r < 2

    @pl.when(source)
    def _():
        for kh in range(2):
            for colour in range(2):
                piece = mc[kh * TK : (kh + 1) * TK, :].T
                gt[kh, colour] = piece[colour * TR : (colour + 1) * TR, :]

    spill = remote(S0, gt.at[1], gall.at[:, (3 - r) & 3, x, zl], dev(jnp.where(r == 0, y - 1, y + 1), x, zl))
    keep0 = pltpu.make_async_copy(gt.at[0], gall.at[:, r, x, zl], loc.at[0])

    @pl.when(source)
    def _():
        spill.start()
        keep0.start()
        keep0.wait()

    shard = gall.at[:, r, x, zl]

    @pl.when(jnp.logical_not(source))
    def _():
        remote(S0, gt.at[1], shard, partner).wait_recv()

    across = remote(S1, shard, shard, dev(y, x, 1 - zl))
    across.start()
    rows_out = remote(
        ZX,
        child_ref.at[0, pl.ds(pl.multiple_of((1 - half) * (CB // 2 * BS), BS), CB // 2 * BS), :],
        recvc,
        partner,
    )
    rows_out.start()

    def slot(c, a, b):
        return gall.at[0, b & 3, a & 3] if c == 0 else gall.at[1, a & 3, b & 3]

    mya, myb = (x, r), (r, x)

    def toward(c, dim, delta):
        along_x = (c == 0) == (dim == 1)
        return dev(y, x + delta, zl) if along_x else dev(y + delta, x, zl)

    SL = (0, -1, 1, 2)

    def ring1(c, hop, d):
        step = 1 - 2 * d
        a, b = mya[c], myb[c]
        k = c * 20 + hop * 2 + d
        if hop == 0:
            return lambda: remote(k, slot(c, a, b), slot(c, a, b), toward(c, 1, step)), slot(c, a - step, b), k
        s = slot(c, a - step, b).at[d]
        return lambda: remote(k, s, s, toward(c, 1, step)), slot(c, a - 2 * step, b).at[d], k

    def ring2(c, si, hop, d):
        step = 1 - 2 * d
        a, b = mya[c] + SL[si], myb[c]
        k = c * 20 + 4 + si * 4 + hop * 2 + d
        if hop == 0:
            return lambda: remote(k, slot(c, a, b), slot(c, a, b), toward(c, 2, step)), slot(c, a, b - step), k
        s = slot(c, a, b - step).at[d]
        return lambda: remote(k, s, s, toward(c, 2, step)), slot(c, a, b - 2 * step).at[d], k

    def start(op):
        op[0]().start()

    def arrived(op):
        remote(op[2], op[1], op[1], partner).wait_recv()

    both = [(c, d) for d in range(2) for c in range(2)]

    def level0():
        remote(S1, shard, gall.at[:, r, x, 1 - zl], partner).wait_recv()
        for c, d in both:
            start(ring1(c, 0, d))
        for c, d in both:
            start(ring2(c, 0, 0, d))

    def level1():
        for c, d in both:
            arrived(ring1(c, 0, d))
            start(ring1(c, 1, d))
            for e in range(2):
                start(ring2(c, 1 + d, 0, e))

    def forward(si):
        def run():
            for c, d in both:
                arrived(ring2(c, si, 0, d))
                start(ring2(c, si, 1, d))

        return run

    def level3():
        for c in range(2):
            for d in range(2):
                arrived(ring1(c, 1, d))
            for e in range(2):
                start(ring2(c, 3, 0, e))

    events = [level0, level1, forward(0), level3, forward(1), forward(2), forward(3)]

    pivot_in.wait_recv()
    for w1 in range(1, 5):

        def unpack(i, carry, w1=w1):
            d = (w1 - 1) * 16 + i
            lo = pl.multiple_of(8 * d, 8)
            hi = pl.multiple_of(PV - 8 - 8 * d, 8)
            pm[pl.ds(lo, 8), 0 : w1 * BS] = rp[d, :, 0 : w1 * BS]
            pm[pl.ds(hi, 8), 0 : (9 - w1) * BS] = rp[d, :, w1 * BS : TRI]
            return carry

        lax.fori_loop(0, 16, unpack, 0)

    rowi = lax.broadcasted_iota(jnp.int32, (BS, BS), 0)
    coli = lax.broadcasted_iota(jnp.int32, (BS, BS), 1)
    eye = (rowi == coli).astype(jnp.float32)

    def panel(k, carry):
        kk = pl.multiple_of(k * BS, BS)
        kr = pl.ds(kk, BS)

        def trail(i, c):
            ir = pl.ds(pl.multiple_of(i * BS, BS), BS)
            tcol[ir, :] = pm[ir, kr] - contract(l_ref[ir, :], l_ref[kr, :], ((1,), (1,)))
            return c

        lax.fori_loop(k, PB, trail, 0)
        dy[:, 0:BS] = tcol[kr, :]
        dy[:, BS:] = eye
        factor_block(dy, uy)
        inv = uy[:, BS:]
        rest = mc[kr, :] - contract(l_ref[kr, :], mc[...], ((1,), (0,)))
        mc[kr, :] = contract(inv, rest, ((1,), (0,)))
        dinv[k] = inv
        l_ref[kr, kr] = uy[:, 0:BS].T

        def below(i, c):
            ir = pl.ds(pl.multiple_of(i * BS, BS), BS)
            l_ref[ir, kr] = contract(tcol[ir, :], inv, ((1,), (1,)))
            return c

        lax.fori_loop(k + 1, PB, below, 0)
        for n, event in enumerate(events):
            pl.when(k == n)(event)
        return carry

    lax.fori_loop(0, PB, panel, 0)

    for j in range(OWN):
        for p in range(PB):
            rows, cols = slice(p * BS, (p + 1) * BS), slice(j * BS, (j + 1) * BS)
            unit = eye * coef_ref[UNIT + PB * j + p]
            mc[rows, cols] = mc[rows, cols] * coef_ref[PLAIN + j] + unit
    w_ref[...] = jnp.zeros_like(w_ref)

    def back(n, carry):
        k = PB - 1 - n
        kr = pl.ds(pl.multiple_of(k * BS, BS), BS)
        rest = mc[kr, :] - contract(l_ref[:, kr], w_ref[...], ((0,), (0,)))
        w_ref[kr, :] = contract(dinv[k], rest, ((0,), (0,)))
        return carry

    lax.fori_loop(0, PB, back, 0)

    for c, d in both:
        for si in range(4):
            arrived(ring2(c, si, 1, d))
    remote(ZX, recvc, recvc, partner).wait_recv()
    swap.wait_send()
    rows_in.wait_send()
    pivot_in.wait_send()

    @pl.when(source)
    def _():
        spill.wait_send()

    across.wait_send()
    rows_out.wait_send()
    for c, d in both:
        for hop in range(2):
            ring1(c, hop, d)[0]().wait_send()
            for si in range(4):
                ring2(c, si, hop, d)[0]().wait_send()


def finish(ids, at_ref, map_ref, g0, g1, w_ref, l_ref, own, other, out, whi, wlo):
    half, grid = ids[0], ids[1]
    i = pl.program_id(0)

    @pl.when(i == 0)
    def _():
        hi = w_ref[...].astype(jnp.bfloat16)
        whi[...] = hi
        wlo[...] = (w_ref[...] - hi.astype(jnp.float32)).astype(jnp.bfloat16)

    def dot(a, b):
        return jnp.dot(a, b, preferred_element_type=jnp.float32)

    for colour in range(2):
        total = jnp.zeros((TR, FW), jnp.float32)
        for part, ref in enumerate((g0, g1)):
            a = ref[colour].reshape(TR, TK)
            hi = a.astype(jnp.bfloat16)
            lo = (a - hi.astype(jnp.float32)).astype(jnp.bfloat16)
            rows = slice(part * TK, (part + 1) * TK)
            total += dot(hi, whi[rows, :]) + dot(hi, wlo[rows, :]) + dot(lo, whi[rows, :])
        out[colour * TR : (colour + 1) * TR, :] = -total

    tile = half * (GRID // 2) + i

    def place(group, nat):
        at = jnp.int32(0)
        for s in range(1, OWN):
            at += jnp.where(at_ref[group * OWN + s] == nat, s, 0)
        return pl.multiple_of(at * BS, BS)

    for c, ref in ((half, own), (1 - half, other)):
        for a in range(HELD):
            row_nat = map_ref[c, tile * HELD + a]
            row = place(tile, row_nat)
            for t in range(HELD):
                col_nat = map_ref[c, grid * HELD + t]
                col = place(grid, col_nat)

                @pl.when((row_nat >= PB) & (col_nat >= PB))
                def _(ref=ref, a=a, t=t, row=row, col=col):
                    where = (pl.ds(row, BS), pl.ds(col, BS))
                    out[where] += ref[a * BS : (a + 1) * BS, t * BS : (t + 1) * BS]

    for s in range(OWN):
        f = at_ref[tile * OWN + s]

        @pl.when(f < PB)
        def _(s=s, f=f):
            rows = pl.ds(pl.multiple_of(f * BS, BS), BS)
            for j in range(OWN):
                q = at_ref[grid * OWN + j]
                cols = pl.ds(pl.multiple_of(jnp.minimum(q, PB - 1) * BS, BS), BS)
                out[s * BS : (s + 1) * BS, j * BS : (j + 1) * BS] = jnp.where(
                    q < PB, l_ref[rows, cols], 0.0
                )


def body(child_blocks, child_map, block_at, pattern):
    f32 = jnp.float32
    vmem = pl.BlockSpec(memory_space=pltpu.VMEM)
    smem = pl.BlockSpec(memory_space=pltpu.SMEM)
    hbm = pl.BlockSpec(memory_space=pltpu.HBM)
    x, xp, source, coef = pl.pallas_call(
        pick_rows,
        name="pick_rows",
        out_shape=(
            jax.ShapeDtypeStruct((PV, CW), f32),
            jax.ShapeDtypeStruct((PEERS, 16, CW), f32),
            jax.ShapeDtypeStruct((2 * PB,), jnp.int32),
            jax.ShapeDtypeStruct((COEFS,), f32),
        ),
        in_specs=[smem, smem, smem, hbm],
        out_specs=(vmem, vmem, smem, smem),
        scratch_shapes=[pltpu.SMEM((2 * PB,), jnp.int32), pltpu.SemaphoreType.DMA((PB,))],
    )(child_map, block_at, pattern, child_blocks)

    gall, recvc, w, low = pl.pallas_call(
        exchange,
        name="exchange",
        out_shape=(
            jax.ShapeDtypeStruct((2, 4, 4, 2, TR, TK), f32),
            jax.ShapeDtypeStruct((CB // 2 * BS, CW), f32),
            jax.ShapeDtypeStruct((PV, FW), f32),
            jax.ShapeDtypeStruct((PV, PV), f32),
        ),
        in_specs=[smem, smem, vmem, vmem, hbm],
        out_specs=(hbm, hbm, vmem, vmem),
        scratch_shapes=[
            pltpu.VMEM((PV, CW), f32),
            pltpu.VMEM((PEERS, 16, CW), f32),
            pltpu.VMEM((8, TRI), f32),
            pltpu.VMEM((PEERS, 8, TRI), f32),
            pltpu.VMEM((PV, FW), f32),
            pltpu.VMEM((2, 2, TR, TK), f32),
            pltpu.VMEM((PV, PV), f32),
            pltpu.VMEM((PB, BS, BS), f32),
            pltpu.VMEM((BS, 2 * BS), f32),
            pltpu.VMEM((BS, 2 * BS), f32),
            pltpu.VMEM((PV, BS), f32),
            pltpu.SemaphoreType.DMA((44,)),
            pltpu.SemaphoreType.DMA((44,)),
            pltpu.SemaphoreType.DMA((2,)),
            pltpu.SemaphoreType.DMA((2,)),
            pltpu.SemaphoreType.DMA((1,)),
        ],
        compiler_params=pltpu.CompilerParams(has_side_effects=True, vmem_limit_bytes=40 * MIB),
    )(source, coef, x, xp, child_blocks)

    ids = jnp.stack([lax.axis_index("half"), lax.axis_index("grid")]).astype(jnp.int32)
    tile = (2, None, None, None, TR, TK)
    whole = lambda i, *_: (0, 0)
    return pl.pallas_call(
        finish,
        name="finish",
        out_shape=jax.ShapeDtypeStruct((NB // 2 * BS, FW), f32),
        grid_spec=pltpu.PrefetchScalarGridSpec(
            num_scalar_prefetch=3,
            grid=(GRID // 2,),
            in_specs=[
                pl.BlockSpec(tile, lambda i, *_: (0, i // 8, (i // 2) % 4, i % 2, 0, 0)),
                pl.BlockSpec(tile, lambda i, *_: (0, 3 - i // 8, (i // 2) % 4, i % 2, 0, 0)),
                pl.BlockSpec((PV, FW), whole, pipeline_mode=pl.Buffered(1)),
                pl.BlockSpec((PV, PV), whole, pipeline_mode=pl.Buffered(1)),
                pl.BlockSpec((None, CW, CW), lambda i, ids, *_: (0, ids[0] * (GRID // 2) + i, 0)),
                pl.BlockSpec((CW, CW), lambda i, *_: (i, 0)),
            ],
            out_specs=pl.BlockSpec((FW, FW), lambda i, *_: (i, 0)),
            scratch_shapes=[pltpu.VMEM((PV, FW), jnp.bfloat16)] * 2,
        ),
        compiler_params=pltpu.CompilerParams(vmem_limit_bytes=40 * MIB),
    )(ids, block_at, child_map, gall, gall, w, low, child_blocks, recvc)


def solution(mesh):
    return jax.shard_map(
        body,
        mesh=mesh,
        in_specs=(P(("cube", "half"), None, "grid"), P("cube", None), P("cube"), P("cube", None)),
        out_specs=P(("cube", "half"), "grid"),
        check_vma=False,
    )
```

```python
import jax
import jax.numpy as jnp
from jax import lax
from jax.experimental import pallas as pl
from jax.experimental.pallas import tpu as pltpu
from jax.sharding import PartitionSpec as P

BS = 128
PB = 8
PV = PB * BS
OWN = 3
HELD = 2
CW = HELD * BS
FW = OWN * BS
GRID = 32
PEERS = 2 * GRID
CB = 64
NB = 96
TR = FW // 2
TK = PV // 2
TRI = (PB + 1) * BS
MESH = pl.DeviceIdType.MESH
HI = lax.Precision.HIGHEST
MIB = 1 << 20


def contract(a, b, dims):
    return lax.dot_general(
        a, b, (dims, ((), ())), precision=HI, preferred_element_type=jnp.float32
    )


SECOND, COLUMN, KEEP, PLAIN, UNIT, COEFS = 0, 16, 28, 52, 55, 80


def pick_rows(map_ref, at_ref, pat_ref, child_ref, x_ref, xp_ref, from_ref, coef_ref, found, sems):
    half = lax.axis_index("half")
    grid = lax.axis_index("grid")

    def scan(b, carry):
        for c in range(2):
            f = map_ref[c, b]

            @pl.when(f < PB)
            def _():
                found[c * PB + f] = b

        return carry

    lax.fori_loop(0, CB, scan, 0)

    def copy(p):
        b = found[half * PB + p]
        return pltpu.make_async_copy(
            child_ref.at[0, pl.ds(pl.multiple_of(b * BS, BS), BS), :],
            x_ref.at[pl.ds(p * BS, BS), :],
            sems.at[p],
        )

    for p in range(PB):
        copy(p).start()
    for c in range(2):
        for p in range(PB):
            b = found[c * PB + p]
            from_ref[c * PB + p] = c * GRID + (b >> 1)
            coef_ref[SECOND + c * PB + p] = (b & 1).astype(jnp.float32)
    for j in range(OWN):
        q = at_ref[grid * OWN + j]
        for t in range(HELD):
            for side in range(2):
                hit = map_ref[jnp.where(side == 0, half, 1 - half), grid * HELD + t] == q
                coef_ref[COLUMN + 4 * j + 2 * t + side] = jnp.where(hit, 1.0, 0.0)
        for p in range(PB):
            keep = jnp.where(q < PB, 1, pat_ref[jnp.maximum(q - PB, 0), p])
            coef_ref[KEEP + PB * j + p] = keep.astype(jnp.float32)
            coef_ref[UNIT + PB * j + p] = jnp.where(q == p, -1.0, 0.0)
        coef_ref[PLAIN + j] = jnp.where(q < PB, 0.0, 1.0)
    for p in range(PB):
        copy(p).wait()
    for d in range(PEERS):
        xp_ref[d, 0:8, :] = x_ref[8 * d : 8 * d + 8, :]
        xp_ref[d, 8:16, :] = x_ref[PV - 8 * d - 8 : PV - 8 * d, :]


def factor_block(dy, out):
    sub = lax.broadcasted_iota(jnp.int32, (8, BS), 0)
    lane = lax.broadcasted_iota(jnp.int32, (8, BS), 1)
    for q in range(BS // 8):
        j0 = 8 * q
        ra = dy[j0 : j0 + 8, 0:BS]
        ry = dy[j0 : j0 + 8, BS : 2 * BS]
        cols = [jnp.broadcast_to(ra[:, j0 + r : j0 + r + 1], (8, BS)) for r in range(8)]
        scale = jnp.ones((8, BS), jnp.float32)
        for r in range(8):
            inv = lax.rsqrt(cols[r][r : r + 1, :])
            scale = jnp.where(sub == r, inv, scale)
            if r == 7:
                break
            part = jnp.where(sub > r, cols[r] * (inv * inv), 0.0)
            for c in range(r + 1, 8):
                cols[c] = cols[c] - part * cols[c][r : r + 1, :]
            ra = ra - part * ra[r : r + 1, :]
            ry = ry - part * ry[r : r + 1, :]
        ra = jnp.where(lane >= sub + j0, ra * scale, 0.0)
        ry = ry * scale
        both = jnp.concatenate([ra, ry], axis=1)
        out[j0 : j0 + 8, :] = both
        if q < BS // 8 - 1:
            step = contract(ra, both, ((0,), (0,)))
            dy[j0 + 8 :, :] = dy[j0 + 8 :, :] - step[j0 + 8 :, :]


def exchange(
    from_ref, coef_ref, x_ref, xp_ref, child_ref,
    u_ref, recvc, l_ref,
    gall, xo, ra, pk, rp, mc, gt, pm, dinv, dy, uy, tcol,
    lhi, llo, vhi, vlo, whi, wlo, stage_out,
    ss, rs, bs, br, psend, precv, loc,
):
    cube = lax.axis_index("cube")
    half = lax.axis_index("half")
    grid = lax.axis_index("grid")
    me = half * GRID + grid
    y, x, zl = grid >> 3, (grid >> 1) & 3, grid & 1
    r = (y - 2 * half) & 3

    def dev(yy, xx, zz):
        return (cube, half, (yy & 3) * 8 + (xx & 3) * 2 + zz)

    partner = (cube, 1 - half, grid)

    def remote(k, src, dst, to):
        return pltpu.make_async_remote_copy(
            src_ref=src, dst_ref=dst, send_sem=ss.at[k], recv_sem=rs.at[k],
            device_id=to, device_id_type=MESH,
        )

    S0, S1, ZX, XS = 60, 61, 62, (63, 64)
    z = half * 2 + zl

    def at(yy, xx, zz):
        return (cube, (zz & 3) >> 1, (yy & 3) * 8 + (xx & 3) * 2 + (zz & 1))

    barrier = pltpu.get_barrier_semaphore()

    def greet(i, carry):
        to = (me + i) & (PEERS - 1)
        pl.semaphore_signal(
            barrier, inc=1, device_id=(cube, to >> 5, to & (GRID - 1)), device_id_type=MESH
        )
        return carry

    lax.fori_loop(1, PEERS, greet, 0)
    pl.semaphore_wait(barrier, PEERS - 1)

    PARTS = (pl.ds(0, TK), pl.ds(TK, TK))
    swap = [remote(XS[kh], x_ref.at[PARTS[kh]], xo.at[PARTS[kh]], partner) for kh in range(2)]
    swap[1].start()
    swap[0].start()

    def spread_rows(i, carry):
        to = (me + i) & (PEERS - 1)
        pltpu.make_async_remote_copy(
            src_ref=xp_ref.at[to], dst_ref=ra.at[me], send_sem=psend.at[0], recv_sem=precv.at[0],
            device_id=(cube, to >> 5, to & (GRID - 1)), device_id_type=MESH,
        ).start()
        return carry

    lax.fori_loop(1, PEERS, spread_rows, 0)
    ra[me] = xp_ref[me]
    rows_in = pltpu.make_async_remote_copy(
        src_ref=xp_ref.at[pl.ds(0, PEERS - 1)], dst_ref=ra.at[pl.ds(0, PEERS - 1)],
        send_sem=psend.at[0], recv_sem=precv.at[0], device_id=partner, device_id_type=MESH,
    )
    for ref in (l_ref, lhi, llo, vhi, vlo, whi, wlo):
        ref[...] = jnp.zeros_like(ref)
    rows_in.wait_recv()

    first = (me >> 4) + 1
    for k in range(PB + 1):
        low = k < first
        p = jnp.where(low, k, k - first)
        total = jnp.zeros((8, BS), jnp.float32)
        for c in range(2):
            came = ra[from_ref[c * PB + p]]
            second = coef_ref[SECOND + c * PB + p]
            came = jnp.where(low, came[0:8, :], came[8:16, :])
            total = total + came[:, 0:BS] * (1.0 - second) + came[:, BS:] * second
        pk[k // 3, :, k % 3 * BS : (k % 3 + 1) * BS] = total

    here = (z, x, y)
    ORDER = ((0, 1, 2), (1, 2, 0), (2, 0, 1))

    def bundle(part, stage, coords):
        d0, d1, d2 = ORDER[part]
        if stage == 0:
            return rp.at[part, pl.ds(coords[d2] * 16 + coords[d1] * 4 + coords[d0], 1)]
        if stage == 1:
            return rp.at[part, pl.ds(coords[d2] * 16 + coords[d1] * 4, 4)]
        return rp.at[part, pl.ds(coords[d2] * 16, 16)]

    def moved(axis, by):
        return tuple((c + by) & 3 if n == axis else c for n, c in enumerate(here))

    def relay(part, stage, by, arriving):
        axis = ORDER[part][stage]
        k = (stage * 3 + part) * 3 + by - 1
        to = moved(axis, by)
        region = bundle(part, stage, moved(axis, -by) if arriving else here)
        return pltpu.make_async_remote_copy(
            src_ref=region, dst_ref=region, send_sem=bs.at[k], recv_sem=br.at[k],
            device_id=at(to[2], to[1], to[0]), device_id_type=MESH,
        )

    RELAYS = [(part, by) for part in range(3) for by in range(1, 4)]

    def relay_start(stage):
        for part, by in RELAYS:
            relay(part, stage, by, False).start()

    def relay_wait(stage):
        for part, by in RELAYS:
            relay(part, stage, by, True).wait_recv()

    for part in range(3):
        d0, d1, d2 = ORDER[part]
        rp[part, here[d2] * 16 + here[d1] * 4 + here[d0]] = pk[part]
    relay_start(0)

    source = r < 2

    def assemble_part(kh):
        swap[kh].wait_recv()
        for j in range(OWN):

            def assemble(p, carry, j=j):
                rows = pl.ds(pl.multiple_of(p * BS, BS), BS)
                keep = coef_ref[KEEP + PB * j + p]
                total = jnp.zeros((BS, BS), jnp.float32)
                for t in range(HELD):
                    cols = slice(t * BS, (t + 1) * BS)
                    total += x_ref[rows, cols] * coef_ref[COLUMN + 4 * j + 2 * t]
                    total += xo[rows, cols] * coef_ref[COLUMN + 4 * j + 2 * t + 1]
                mc[rows, j * BS : (j + 1) * BS] = total * keep
                return carry

            lax.fori_loop(kh * PB // 2, (kh + 1) * PB // 2, assemble, 0)

    shard = gall.at[:, r, x, zl]
    spill = remote(S0, gt, gall.at[:, (3 - r) & 3, x, zl], dev(jnp.where(r == 0, y - 1, y + 1), x, zl))
    across = remote(S1, shard, shard, dev(y, x, 1 - zl))

    assemble_part(1)

    @pl.when(source)
    def _():
        piece = mc[TK:PV, :].T
        for colour in range(2):
            gt[colour] = piece[colour * TR : (colour + 1) * TR, :]
        spill.start()

    relay_wait(0)
    relay_start(1)
    assemble_part(0)

    @pl.when(source)
    def _():
        piece = mc[0:TK, :].T
        for colour in range(2):
            gall[colour, r, x, zl] = piece[colour * TR : (colour + 1) * TR, :]

    relay_wait(1)
    relay_start(2)

    @pl.when(jnp.logical_not(source))
    def _():
        remote(S0, gt, shard, partner).wait_recv()

    def slot(c, a, b, n):
        level = zl if n == 0 else 1 - zl
        return gall.at[0, b & 3, a & 3, level] if c == 0 else gall.at[1, a & 3, b & 3, level]

    mya, myb = (x, r), (r, x)
    turn = (zl, 1 - zl)

    def toward(c, dim, delta):
        along_x = (c == 0) == (dim == 1)
        return dev(y, x + delta, zl) if along_x else dev(y + delta, x, zl)

    SL = (0, -1, 1, 2)

    def lane1(c, n, d):
        step = 1 - 2 * d
        s = slot(c, mya[c], myb[c], n)
        return s, slot(c, mya[c] - step, myb[c], n), toward(c, 1, step), c * 30 + n * 15 + d

    def lane1far(c, n):
        step = 1 - 2 * turn[n]
        a, b = mya[c], myb[c]
        return slot(c, a - step, b, n), slot(c, a - 2 * step, b, n), toward(c, 1, step), c * 30 + n * 15 + 2

    def lane2(c, n, si, d):
        step = 1 - 2 * d
        a, b = mya[c] + SL[si], myb[c]
        k = c * 30 + n * 15 + 3 + si * 3 + d
        return slot(c, a, b, n), slot(c, a, b - step, n), toward(c, 2, step), k

    def lane2far(c, n, si):
        step = 1 - 2 * turn[n]
        a, b = mya[c] + SL[si], myb[c]
        k = c * 30 + n * 15 + 3 + si * 3 + 2
        return slot(c, a, b - step, n), slot(c, a, b - 2 * step, n), toward(c, 2, step), k

    def start(lane):
        remote(lane[3], lane[0], lane[0], lane[2]).start()

    def arrived(lane):
        remote(lane[3], lane[1], lane[1], partner).wait_recv()

    def sent(lane):
        remote(lane[3], lane[0], lane[0], lane[2]).wait_send()

    def own_ready(n):
        def run():
            if n == 1:
                remote(S1, shard, gall.at[:, r, x, 1 - zl], partner).wait_recv()
            for d in range(2):
                for c in range(2):
                    start(lane1(c, n, d))
            for d in range(2):
                for c in range(2):
                    start(lane2(c, n, 0, d))

        return run

    def near(n):
        def run():
            for c in range(2):
                for d in range(2):
                    arrived(lane1(c, n, d))
                start(lane1far(c, n))
            for si in (1, 2):
                for d in range(2):
                    for c in range(2):
                        start(lane2(c, n, si, d))

        return run

    def far(n):
        def run():
            for c in range(2):
                arrived(lane1far(c, n))
                for d in range(2):
                    start(lane2(c, n, 3, d))

        return run

    def forward(n, si):
        def run():
            for c in range(2):
                for d in range(2):
                    arrived(lane2(c, n, si, d))
                start(lane2far(c, n, si))

        return run

    across.start()
    own_ready(0)()
    rows_out = remote(
        ZX,
        child_ref.at[0, pl.ds(pl.multiple_of((1 - half) * (CB // 2 * BS), BS), CB // 2 * BS), :],
        recvc,
        partner,
    )
    rows_out.start()

    events = {
        (0, 0): [own_ready(1)],
        (0, 1): [near(0)],
        (1, 0): [forward(0, 0)],
        (1, 1): [near(1)],
        (2, 1): [forward(1, 0)],
        (3, 0): [far(0)],
        (4, 0): [far(1)],
        (4, 1): [forward(0, 1)],
        (5, 0): [forward(0, 2)],
        (6, 0): [forward(1, 1)],
        (6, 1): [forward(1, 2)],
        (7, 1): [forward(0, 3)],
    }

    def follow(k, part):
        for (step, at_part), todo in events.items():
            if at_part == part:

                @pl.when(k == step)
                def _(todo=todo):
                    for event in todo:
                        event()

    relay_wait(2)
    for group in range(4):
        w1 = group + 1

        def unpack(i, carry, group=group, w1=w1):
            yy, xx, zz = (group & 1) * 2 + (i >> 3), (i >> 1) & 3, (group >> 1) * 2 + (i & 1)
            d = group * 16 + i
            lo = pl.ds(pl.multiple_of(8 * d, 8), 8)
            hi = pl.ds(pl.multiple_of(PV - 8 - 8 * d, 8), 8)
            index = (yy * 16 + xx * 4 + zz, zz * 16 + yy * 4 + xx, xx * 16 + zz * 4 + yy)
            for k in range(PB + 1):
                share = rp[k // 3, index[k // 3], :, k % 3 * BS : (k % 3 + 1) * BS]
                if k < w1:
                    pm[lo, k * BS : (k + 1) * BS] = share
                else:
                    pm[hi, (k - w1) * BS : (k - w1 + 1) * BS] = share
            return carry

        lax.fori_loop(0, 16, unpack, 0)

    rowi = lax.broadcasted_iota(jnp.int32, (BS, BS), 0)
    coli = lax.broadcasted_iota(jnp.int32, (BS, BS), 1)
    eye = (rowi == coli).astype(jnp.float32)

    def split(ref_hi, ref_lo, where, value):
        top = value.astype(jnp.bfloat16)
        ref_hi[where] = top
        ref_lo[where] = (value - top.astype(jnp.float32)).astype(jnp.bfloat16)

    def three(ahi, alo, bhi, blo, dims):
        def dot(a, b):
            return lax.dot_general(a, b, (dims, ((), ())), preferred_element_type=jnp.float32)

        return dot(ahi, bhi) + dot(ahi, blo) + dot(alo, bhi)

    def panel(k, carry):
        kk = pl.multiple_of(k * BS, BS)
        kr = pl.ds(kk, BS)

        def reduce_by(known):
            def trail(i, c):
                ir = pl.ds(pl.multiple_of(i * BS, BS), BS)
                tcol[ir, :] = pm[ir, kr] - three(
                    lhi[ir, 0:known], llo[ir, 0:known], lhi[kr, 0:known], llo[kr, 0:known], ((1,), (1,))
                )
                return c

            lax.fori_loop(k, PB, trail, 0)
            mc[kr, :] = mc[kr, :] - three(
                lhi[kr, 0:known], llo[kr, 0:known], vhi[0:known, :], vlo[0:known, :], ((1,), (0,))
            )

        pl.when(k < PB // 2)(lambda: reduce_by(TK))
        pl.when(k >= PB // 2)(lambda: reduce_by(PV))

        follow(k, 0)
        dy[:, 0:BS] = tcol[kr, :]
        dy[:, BS:] = eye
        factor_block(dy, uy)
        inv = uy[:, BS:]
        solved = contract(inv, mc[kr, :], ((1,), (0,)))
        mc[kr, :] = solved
        split(vhi, vlo, (kr, slice(None)), solved)
        dinv[k] = inv
        l_ref[kr, kr] = uy[:, 0:BS].T

        def below(i, c):
            ir = pl.ds(pl.multiple_of(i * BS, BS), BS)
            got = contract(tcol[ir, :], inv, ((1,), (1,)))
            l_ref[ir, kr] = got
            split(lhi, llo, (ir, kr), got)
            return c

        lax.fori_loop(k + 1, PB, below, 0)
        follow(k, 1)
        return carry

    lax.fori_loop(0, PB, panel, 0)

    for j in range(OWN):
        for p in range(PB):
            rows, cols = slice(p * BS, (p + 1) * BS), slice(j * BS, (j + 1) * BS)
            unit = eye * coef_ref[UNIT + PB * j + p]
            mc[rows, cols] = mc[rows, cols] * coef_ref[PLAIN + j] + unit

    def back(n, carry):
        k = PB - 1 - n
        kr = pl.ds(pl.multiple_of(k * BS, BS), BS)
        rest = mc[kr, :] - three(lhi[:, kr], llo[:, kr], whi[...], wlo[...], ((0,), (0,)))
        split(whi, wlo, (kr, slice(None)), contract(dinv[k], rest, ((0,), (0,))))
        return carry

    lax.fori_loop(0, PB, back, 0)
    forward(1, 3)()

    def put(turn_at, tile):
        return pltpu.make_async_copy(
            stage_out.at[turn_at], u_ref.at[pl.ds(pl.multiple_of(tile * FW, FW), FW), :], loc.at[turn_at]
        )

    for group in range(4):
        for n in range(2):
            arrived(lane2far(0, n, group))
            if group == 3:
                for si in range(4):
                    arrived(lane2far(1, n, si))
        xx = (x + SL[group]) & 3

        def product(m, carry, group=group, xx=xx):
            yy, zz, turn_at = m >> 1, m & 1, m & 1
            tile = yy * 8 + xx * 2 + zz
            if group > 0:
                put(turn_at, 0).wait()
            else:
                pl.when(m >= 2)(lambda: put(turn_at, 0).wait())
            for colour in range(2):
                total = jnp.zeros((TR, FW), jnp.float32)
                for part, row in enumerate((yy, 3 - yy)):
                    value = gall[colour, row, xx, zz]
                    top = value.astype(jnp.bfloat16)
                    rest = (value - top.astype(jnp.float32)).astype(jnp.bfloat16)
                    rows = slice(part * TK, (part + 1) * TK)
                    total += three(top, rest, whi[rows, :], wlo[rows, :], ((1,), (0,)))
                stage_out[turn_at, colour * TR : (colour + 1) * TR, :] = total
            put(turn_at, tile).start()
            return carry

        lax.fori_loop(0, 4, product, 0)
    for turn_at in range(2):
        put(turn_at, 0).wait()

    ALL = [(c, n) for c in range(2) for n in range(2)]
    remote(ZX, recvc, recvc, partner).wait_recv()
    for part in swap:
        part.wait_send()
    rows_in.wait_send()
    for stage in range(3):
        for part, by in RELAYS:
            relay(part, stage, by, False).wait_send()

    @pl.when(source)
    def _():
        spill.wait_send()

    across.wait_send()
    rows_out.wait_send()
    for c, n in ALL:
        sent(lane1far(c, n))
        for d in range(2):
            sent(lane1(c, n, d))
        for si in range(4):
            sent(lane2far(c, n, si))
            for d in range(2):
                sent(lane2(c, n, si, d))


def finish(ids, at_ref, map_ref, u_ref, l_ref, own, other, out):
    half, grid = ids[0], ids[1]
    i = pl.program_id(0)
    out[...] = -u_ref[...]

    tile = half * (GRID // 2) + i

    def place(group, nat):
        at = jnp.int32(0)
        for s in range(1, OWN):
            at += jnp.where(at_ref[group * OWN + s] == nat, s, 0)
        return pl.multiple_of(at * BS, BS)

    for c, ref in ((half, own), (1 - half, other)):
        for a in range(HELD):
            row_nat = map_ref[c, tile * HELD + a]
            row = place(tile, row_nat)
            for t in range(HELD):
                col_nat = map_ref[c, grid * HELD + t]
                col = place(grid, col_nat)

                @pl.when((row_nat >= PB) & (col_nat >= PB))
                def _(ref=ref, a=a, t=t, row=row, col=col):
                    where = (pl.ds(row, BS), pl.ds(col, BS))
                    out[where] += ref[a * BS : (a + 1) * BS, t * BS : (t + 1) * BS]

    for s in range(OWN):
        f = at_ref[tile * OWN + s]

        @pl.when(f < PB)
        def _(s=s, f=f):
            rows = pl.ds(pl.multiple_of(f * BS, BS), BS)
            for j in range(OWN):
                q = at_ref[grid * OWN + j]
                cols = pl.ds(pl.multiple_of(jnp.minimum(q, PB - 1) * BS, BS), BS)
                out[s * BS : (s + 1) * BS, j * BS : (j + 1) * BS] = jnp.where(
                    q < PB, l_ref[rows, cols], 0.0
                )


def body(child_blocks, child_map, block_at, pattern):
    f32 = jnp.float32
    vmem = pl.BlockSpec(memory_space=pltpu.VMEM)
    smem = pl.BlockSpec(memory_space=pltpu.SMEM)
    hbm = pl.BlockSpec(memory_space=pltpu.HBM)
    x, xp, source, coef = pl.pallas_call(
        pick_rows,
        name="pick_rows",
        out_shape=(
            jax.ShapeDtypeStruct((PV, CW), f32),
            jax.ShapeDtypeStruct((PEERS, 16, CW), f32),
            jax.ShapeDtypeStruct((2 * PB,), jnp.int32),
            jax.ShapeDtypeStruct((COEFS,), f32),
        ),
        in_specs=[smem, smem, smem, hbm],
        out_specs=(vmem, vmem, smem, smem),
        scratch_shapes=[pltpu.SMEM((2 * PB,), jnp.int32), pltpu.SemaphoreType.DMA((PB,))],
    )(child_map, block_at, pattern, child_blocks)

    u, recvc, low = pl.pallas_call(
        exchange,
        name="exchange",
        out_shape=(
            jax.ShapeDtypeStruct((NB // 2 * BS, FW), f32),
            jax.ShapeDtypeStruct((CB // 2 * BS, CW), f32),
            jax.ShapeDtypeStruct((PV, PV), f32),
        ),
        in_specs=[smem, smem, vmem, vmem, hbm],
        out_specs=(hbm, hbm, vmem),
        scratch_shapes=[
            pltpu.VMEM((2, 4, 4, 2, TR, TK), f32),
            pltpu.VMEM((PV, CW), f32),
            pltpu.VMEM((PEERS, 16, CW), f32),
            pltpu.VMEM((3, 8, TRI // 3), f32),
            pltpu.VMEM((3, PEERS, 8, TRI // 3), f32),
            pltpu.VMEM((PV, FW), f32),
            pltpu.VMEM((2, TR, TK), f32),
            pltpu.VMEM((PV, PV), f32),
            pltpu.VMEM((PB, BS, BS), f32),
            pltpu.VMEM((BS, 2 * BS), f32),
            pltpu.VMEM((BS, 2 * BS), f32),
            pltpu.VMEM((PV, BS), f32),
            *[pltpu.VMEM((PV, PV), jnp.bfloat16)] * 2,
            *[pltpu.VMEM((PV, FW), jnp.bfloat16)] * 4,
            pltpu.VMEM((2, FW, FW), f32),
            pltpu.SemaphoreType.DMA((65,)),
            pltpu.SemaphoreType.DMA((65,)),
            pltpu.SemaphoreType.DMA((27,)),
            pltpu.SemaphoreType.DMA((27,)),
            pltpu.SemaphoreType.DMA((1,)),
            pltpu.SemaphoreType.DMA((1,)),
            pltpu.SemaphoreType.DMA((2,)),
        ],
        compiler_params=pltpu.CompilerParams(
            has_side_effects=True, collective_id=0, vmem_limit_bytes=60 * MIB
        ),
    )(source, coef, x, xp, child_blocks)

    ids = jnp.stack([lax.axis_index("half"), lax.axis_index("grid")]).astype(jnp.int32)
    return pl.pallas_call(
        finish,
        name="finish",
        out_shape=jax.ShapeDtypeStruct((NB // 2 * BS, FW), f32),
        grid_spec=pltpu.PrefetchScalarGridSpec(
            num_scalar_prefetch=3,
            grid=(GRID // 2,),
            in_specs=[
                pl.BlockSpec((FW, FW), lambda i, *_: (i, 0)),
                pl.BlockSpec((PV, PV), lambda i, *_: (0, 0), pipeline_mode=pl.Buffered(1)),
                pl.BlockSpec((None, CW, CW), lambda i, ids, *_: (0, ids[0] * (GRID // 2) + i, 0)),
                pl.BlockSpec((CW, CW), lambda i, *_: (i, 0)),
            ],
            out_specs=pl.BlockSpec((FW, FW), lambda i, *_: (i, 0)),
        ),
        compiler_params=pltpu.CompilerParams(vmem_limit_bytes=24 * MIB),
    )(ids, block_at, child_map, u, low, child_blocks, recvc)


def solution(mesh):
    return jax.shard_map(
        body,
        mesh=mesh,
        in_specs=(P(("cube", "half"), None, "grid"), P("cube", None), P("cube"), P("cube", None)),
        out_specs=P(("cube", "half"), "grid"),
        check_vma=False,
    )
```

```python
import jax
import jax.numpy as jnp
from jax import lax
from jax.experimental import pallas as pl
from jax.experimental.pallas import tpu as pltpu
from jax.sharding import PartitionSpec as P

BS = 128
PB = 8
PV = PB * BS
OWN = 3
HELD = 2
CW = HELD * BS
FW = OWN * BS
GRID = 32
PEERS = 2 * GRID
CB = 64
NB = 96
TR = FW // 2
TK = PV // 2
TRI = (PB + 1) * BS
MESH = pl.DeviceIdType.MESH
HI = lax.Precision.HIGHEST
MIB = 1 << 20


def contract(a, b, dims):
    return lax.dot_general(
        a, b, (dims, ((), ())), precision=HI, preferred_element_type=jnp.float32
    )


SECOND, COLUMN, KEEP, PLAIN, UNIT, COEFS = 0, 16, 28, 52, 55, 80


def pick_rows(map_ref, at_ref, pat_ref, child_ref, x_ref, xp_ref, from_ref, coef_ref, found, sems):
    half = lax.axis_index("half")
    grid = lax.axis_index("grid")

    def scan(b, carry):
        for c in range(2):
            f = map_ref[c, b]

            @pl.when(f < PB)
            def _():
                found[c * PB + f] = b

        return carry

    lax.fori_loop(0, CB, scan, 0)

    def copy(p):
        b = found[half * PB + p]
        return pltpu.make_async_copy(
            child_ref.at[0, pl.ds(pl.multiple_of(b * BS, BS), BS), :],
            x_ref.at[pl.ds(p * BS, BS), :],
            sems.at[p],
        )

    for p in range(PB):
        copy(p).start()
    for c in range(2):
        for p in range(PB):
            b = found[c * PB + p]
            from_ref[c * PB + p] = c * GRID + (b >> 1)
            coef_ref[SECOND + c * PB + p] = (b & 1).astype(jnp.float32)
    for j in range(OWN):
        q = at_ref[grid * OWN + j]
        for t in range(HELD):
            for side in range(2):
                hit = map_ref[jnp.where(side == 0, half, 1 - half), grid * HELD + t] == q
                coef_ref[COLUMN + 4 * j + 2 * t + side] = jnp.where(hit, 1.0, 0.0)
        for p in range(PB):
            keep = jnp.where(q < PB, 1, pat_ref[jnp.maximum(q - PB, 0), p])
            coef_ref[KEEP + PB * j + p] = keep.astype(jnp.float32)
            coef_ref[UNIT + PB * j + p] = jnp.where(q == p, -1.0, 0.0)
        coef_ref[PLAIN + j] = jnp.where(q < PB, 0.0, 1.0)
    for p in range(PB):
        copy(p).wait()
    for d in range(PEERS):
        xp_ref[d, 0:8, :] = x_ref[8 * d : 8 * d + 8, :]
        xp_ref[d, 8:16, :] = x_ref[PV - 8 * d - 8 : PV - 8 * d, :]


def factor_block(dy, out):
    step_rows = 16
    sub = lax.broadcasted_iota(jnp.int32, (step_rows, BS), 0)
    lane = lax.broadcasted_iota(jnp.int32, (step_rows, BS), 1)
    for j0 in range(0, BS, step_rows):
        end = j0 + step_rows
        ra = dy[j0:end, 0:BS]
        ry = dy[j0:end, BS : 2 * BS]
        cols = [
            jnp.broadcast_to(ra[:, j0 + r : j0 + r + 1], (step_rows, BS)) for r in range(step_rows)
        ]
        scale = jnp.ones((step_rows, BS), jnp.float32)
        for r in range(step_rows):
            inv = lax.rsqrt(cols[r][r : r + 1, :])
            scale = jnp.where(sub == r, inv, scale)
            if r == step_rows - 1:
                break
            part = jnp.where(sub > r, cols[r] * (inv * inv), 0.0)
            for c in range(r + 1, step_rows):
                cols[c] = cols[c] - part * cols[c][r : r + 1, :]
            ra = ra - part * ra[r : r + 1, :]
            ry = ry - part * ry[r : r + 1, :]
        ra = jnp.where(lane >= sub + j0, ra * scale, 0.0)
        both = jnp.concatenate([ra, ry * scale], axis=1)
        out[j0:end, :] = both
        if end < BS:
            top = both.astype(jnp.bfloat16)
            rest = (both - top.astype(jnp.float32)).astype(jnp.bfloat16)
            left = jnp.concatenate([top[:, 0:BS], top[:, 0:BS], rest[:, 0:BS]], axis=0)
            right = jnp.concatenate([top, rest, top], axis=0)
            step = lax.dot_general(
                left, right, (((0,), (0,)), ((), ())), preferred_element_type=jnp.float32
            )
            dy[end:, :] = dy[end:, :] - step[end:, :]


def exchange(
    from_ref, coef_ref, x_ref, xp_ref, child_ref,
    u_ref, recvc, l_ref,
    gall, xo, ra, pk, rp, mc, gt, pm, dinv, dy, uy, tcol,
    lhi, llo, vhi, vlo, whi, wlo, stage_out,
    ss, rs, bs, br, psend, precv, loc,
):
    cube = lax.axis_index("cube")
    half = lax.axis_index("half")
    grid = lax.axis_index("grid")
    me = half * GRID + grid
    y, x, zl = grid >> 3, (grid >> 1) & 3, grid & 1
    r = (y - 2 * half) & 3

    def dev(yy, xx, zz):
        return (cube, half, (yy & 3) * 8 + (xx & 3) * 2 + zz)

    partner = (cube, 1 - half, grid)

    def remote(k, src, dst, to):
        return pltpu.make_async_remote_copy(
            src_ref=src, dst_ref=dst, send_sem=ss.at[k], recv_sem=rs.at[k],
            device_id=to, device_id_type=MESH,
        )

    S0, S1, ZX, XS = (60, 61), (62, 63), 64, (65, 66)
    z = half * 2 + zl

    def at(yy, xx, zz):
        return (cube, (zz & 3) >> 1, (yy & 3) * 8 + (xx & 3) * 2 + (zz & 1))

    barrier = pltpu.get_barrier_semaphore()

    def greet(i, carry):
        to = (me + i) & (PEERS - 1)
        pl.semaphore_signal(
            barrier, inc=1, device_id=(cube, to >> 5, to & (GRID - 1)), device_id_type=MESH
        )
        return carry

    lax.fori_loop(1, PEERS, greet, 0)
    for ref in (l_ref, lhi, llo, vhi, vlo, whi, wlo):
        ref[...] = jnp.zeros_like(ref)
    pl.semaphore_wait(barrier, PEERS - 1)

    PARTS = (pl.ds(0, TK), pl.ds(TK, TK))
    swap = [remote(XS[kh], x_ref.at[PARTS[kh]], xo.at[PARTS[kh]], partner) for kh in range(2)]
    swap[1].start()
    swap[0].start()

    def spread_rows(i, carry):
        to = (me + i) & (PEERS - 1)
        pltpu.make_async_remote_copy(
            src_ref=xp_ref.at[to], dst_ref=ra.at[me], send_sem=psend.at[0], recv_sem=precv.at[0],
            device_id=(cube, to >> 5, to & (GRID - 1)), device_id_type=MESH,
        ).start()
        return carry

    lax.fori_loop(1, PEERS, spread_rows, 0)
    ra[me] = xp_ref[me]
    rows_in = pltpu.make_async_remote_copy(
        src_ref=xp_ref.at[pl.ds(0, PEERS - 1)], dst_ref=ra.at[pl.ds(0, PEERS - 1)],
        send_sem=psend.at[0], recv_sem=precv.at[0], device_id=partner, device_id_type=MESH,
    )
    rows_in.wait_recv()

    first = (me >> 4) + 1
    for k in range(PB + 1):
        low = k < first
        p = jnp.where(low, k, k - first)
        total = jnp.zeros((8, BS), jnp.float32)
        for c in range(2):
            came = ra[from_ref[c * PB + p]]
            second = coef_ref[SECOND + c * PB + p]
            came = jnp.where(low, came[0:8, :], came[8:16, :])
            total = total + came[:, 0:BS] * (1.0 - second) + came[:, BS:] * second
        pk[k // 3, :, k % 3 * BS : (k % 3 + 1) * BS] = total

    here = (z, x, y)
    ORDER = ((0, 1, 2), (1, 2, 0), (2, 0, 1))

    def bundle(part, stage, coords):
        d0, d1, d2 = ORDER[part]
        if stage == 0:
            return rp.at[part, pl.ds(coords[d2] * 16 + coords[d1] * 4 + coords[d0], 1)]
        if stage == 1:
            return rp.at[part, pl.ds(coords[d2] * 16 + coords[d1] * 4, 4)]
        return rp.at[part, pl.ds(coords[d2] * 16, 16)]

    def moved(axis, by):
        return tuple((c + by) & 3 if n == axis else c for n, c in enumerate(here))

    def relay(part, stage, by, arriving):
        axis = ORDER[part][stage]
        k = (stage * 3 + part) * 3 + by - 1
        to = moved(axis, by)
        region = bundle(part, stage, moved(axis, -by) if arriving else here)
        return pltpu.make_async_remote_copy(
            src_ref=region, dst_ref=region, send_sem=bs.at[k], recv_sem=br.at[k],
            device_id=at(to[2], to[1], to[0]), device_id_type=MESH,
        )

    RELAYS = [(part, by) for part in range(3) for by in range(1, 4)]

    def relay_start(stage):
        for part, by in RELAYS:
            relay(part, stage, by, False).start()

    def relay_wait(stage):
        for part, by in RELAYS:
            relay(part, stage, by, True).wait_recv()

    for part in range(3):
        d0, d1, d2 = ORDER[part]
        rp[part, here[d2] * 16 + here[d1] * 4 + here[d0]] = pk[part]
    relay_start(0)

    source = r < 2

    def assemble_part(kh):
        swap[kh].wait_recv()
        for j in range(OWN):

            def assemble(p, carry, j=j):
                rows = pl.ds(pl.multiple_of(p * BS, BS), BS)
                keep = coef_ref[KEEP + PB * j + p]
                total = jnp.zeros((BS, BS), jnp.float32)
                for t in range(HELD):
                    cols = slice(t * BS, (t + 1) * BS)
                    total += x_ref[rows, cols] * coef_ref[COLUMN + 4 * j + 2 * t]
                    total += xo[rows, cols] * coef_ref[COLUMN + 4 * j + 2 * t + 1]
                mc[rows, j * BS : (j + 1) * BS] = total * keep
                return carry

            lax.fori_loop(kh * PB // 2, (kh + 1) * PB // 2, assemble, 0)

    def slot(c, a, b, n):
        level = zl if n == 0 else 1 - zl
        return gall.at[0, b & 3, a & 3, level] if c == 0 else gall.at[1, a & 3, b & 3, level]

    mya, myb = (x, r), (r, x)
    turn = (zl, 1 - zl)

    def toward(c, dim, delta):
        along_x = (c == 0) == (dim == 1)
        return dev(y, x + delta, zl) if along_x else dev(y + delta, x, zl)

    SL = (0, -1, 1, 2)

    def lane1(c, n, d):
        step = 1 - 2 * d
        s = slot(c, mya[c], myb[c], n)
        return s, slot(c, mya[c] - step, myb[c], n), toward(c, 1, step), c * 30 + n * 15 + d

    def lane1far(c, n):
        step = 1 - 2 * turn[n]
        a, b = mya[c], myb[c]
        return slot(c, a - step, b, n), slot(c, a - 2 * step, b, n), toward(c, 1, step), c * 30 + n * 15 + 2

    def lane2(c, n, si, d):
        step = 1 - 2 * d
        a, b = mya[c] + SL[si], myb[c]
        k = c * 30 + n * 15 + 3 + si * 3 + d
        return slot(c, a, b, n), slot(c, a, b - step, n), toward(c, 2, step), k

    def lane2far(c, n, si):
        step = 1 - 2 * turn[n]
        a, b = mya[c] + SL[si], myb[c]
        k = c * 30 + n * 15 + 3 + si * 3 + 2
        return slot(c, a, b - step, n), slot(c, a, b - 2 * step, n), toward(c, 2, step), k

    def start(lane):
        remote(lane[3], lane[0], lane[0], lane[2]).start()

    def arrived(lane):
        remote(lane[3], lane[1], lane[1], partner).wait_recv()

    def sent(lane):
        remote(lane[3], lane[0], lane[0], lane[2]).wait_send()

    def own_ready(n, c):
        for d in range(2):
            start(lane1(c, n, d))
            start(lane2(c, n, 0, d))

    def near(n):
        def run():
            for c in range(2):
                for d in range(2):
                    arrived(lane1(c, n, d))
                start(lane1far(c, n))
            for si in (1, 2):
                for d in range(2):
                    for c in range(2):
                        start(lane2(c, n, si, d))

        return run

    def far(n):
        def run():
            for c in range(2):
                arrived(lane1far(c, n))
                for d in range(2):
                    start(lane2(c, n, 3, d))

        return run

    def forward(n, si):
        def run():
            for c in range(2):
                for d in range(2):
                    arrived(lane2(c, n, si, d))
                start(lane2far(c, n, si))

        return run

    shard = [gall.at[c, r, x, zl] for c in range(2)]
    spill = [
        remote(S0[c], gt.at[c], gall.at[c, (3 - r) & 3, x, zl], dev(jnp.where(r == 0, y - 1, y + 1), x, zl))
        for c in range(2)
    ]
    across = [remote(S1[c], shard[c], shard[c], dev(y, x, 1 - zl)) for c in range(2)]

    assemble_part(1)

    @pl.when(source)
    def _():
        piece = mc[TK:PV, :].T
        for c in range(2):
            gt[c] = piece[c * TR : (c + 1) * TR, :]
            spill[c].start()

    relay_wait(0)
    relay_start(1)
    assemble_part(0)

    @pl.when(source)
    def _():
        piece = mc[0:TK, :].T
        for c in range(2):
            gall[c, r, x, zl] = piece[c * TR : (c + 1) * TR, :]
            across[c].start()
            own_ready(0, c)

    relay_wait(1)
    relay_start(2)

    @pl.when(jnp.logical_not(source))
    def _():
        for c in range(2):
            remote(S0[c], gt.at[c], shard[c], partner).wait_recv()
            across[c].start()
            own_ready(0, c)

    rows_out = remote(
        ZX,
        child_ref.at[0, pl.ds(pl.multiple_of((1 - half) * (CB // 2 * BS), BS), CB // 2 * BS), :],
        recvc,
        partner,
    )

    def other_ready():
        for c in range(2):
            remote(S1[c], shard[c], gall.at[c, r, x, 1 - zl], partner).wait_recv()
            own_ready(1, c)

    events = {
        (0, 0): [near(0)],
        (1, 0): [forward(0, 0), rows_out.start],
        (1, 1): [near(1)],
        (2, 1): [forward(1, 0)],
        (3, 1): [far(0)],
        (4, 0): [forward(0, 1)],
        (4, 1): [forward(0, 2)],
        (5, 0): [far(1)],
        (5, 1): [forward(1, 1)],
        (6, 0): [forward(1, 2)],
        (7, 0): [forward(0, 3)],
    }

    def follow(k, part):
        for (step, at_part), todo in events.items():
            if at_part == part:

                @pl.when(k == step)
                def _(todo=todo):
                    for event in todo:
                        event()

    relay_wait(2)
    other_ready()
    for group in range(4):
        w1 = group + 1

        def unpack(i, carry, group=group, w1=w1):
            yy, xx, zz = (group & 1) * 2 + (i >> 3), (i >> 1) & 3, (group >> 1) * 2 + (i & 1)
            d = group * 16 + i
            lo = pl.ds(pl.multiple_of(8 * d, 8), 8)
            hi = pl.ds(pl.multiple_of(PV - 8 - 8 * d, 8), 8)
            index = (yy * 16 + xx * 4 + zz, zz * 16 + yy * 4 + xx, xx * 16 + zz * 4 + yy)
            for k in range(PB + 1):
                share = rp[k // 3, index[k // 3], :, k % 3 * BS : (k % 3 + 1) * BS]
                if k < w1:
                    pm[lo, k * BS : (k + 1) * BS] = share
                else:
                    pm[hi, (k - w1) * BS : (k - w1 + 1) * BS] = share
            return carry

        lax.fori_loop(0, 16, unpack, 0)

    rowi = lax.broadcasted_iota(jnp.int32, (BS, BS), 0)
    coli = lax.broadcasted_iota(jnp.int32, (BS, BS), 1)
    eye = (rowi == coli).astype(jnp.float32)

    def split(ref_hi, ref_lo, where, value):
        top = value.astype(jnp.bfloat16)
        ref_hi[where] = top
        ref_lo[where] = (value - top.astype(jnp.float32)).astype(jnp.bfloat16)

    def three(ahi, alo, bhi, blo, dims):
        def dot(a, b):
            return lax.dot_general(a, b, (dims, ((), ())), preferred_element_type=jnp.float32)

        return dot(ahi, bhi) + dot(ahi, blo) + dot(alo, bhi)

    def panel(k, carry):
        kk = pl.multiple_of(k * BS, BS)
        kr = pl.ds(kk, BS)

        def reduce_by(known):
            def trail(i, c):
                ir = pl.ds(pl.multiple_of(i * BS, BS), BS)
                tcol[ir, :] = pm[ir, kr] - three(
                    lhi[ir, 0:known], llo[ir, 0:known], lhi[kr, 0:known], llo[kr, 0:known], ((1,), (1,))
                )
                return c

            lax.fori_loop(k, PB, trail, 0)
            mc[kr, :] = mc[kr, :] - three(
                lhi[kr, 0:known], llo[kr, 0:known], vhi[0:known, :], vlo[0:known, :], ((1,), (0,))
            )

        pl.when(k < PB // 2)(lambda: reduce_by(TK))
        pl.when(k >= PB // 2)(lambda: reduce_by(PV))

        follow(k, 0)
        dy[:, 0:BS] = tcol[kr, :]
        dy[:, BS:] = eye
        factor_block(dy, uy)
        inv = uy[:, BS:]
        solved = contract(inv, mc[kr, :], ((1,), (0,)))
        mc[kr, :] = solved
        split(vhi, vlo, (kr, slice(None)), solved)
        dinv[k] = inv
        l_ref[kr, kr] = uy[:, 0:BS].T

        def below(i, c):
            ir = pl.ds(pl.multiple_of(i * BS, BS), BS)
            got = contract(tcol[ir, :], inv, ((1,), (1,)))
            l_ref[ir, kr] = got
            split(lhi, llo, (ir, kr), got)
            return c

        lax.fori_loop(k + 1, PB, below, 0)
        follow(k, 1)
        return carry

    lax.fori_loop(0, PB, panel, 0)

    for j in range(OWN):
        for p in range(PB):
            rows, cols = slice(p * BS, (p + 1) * BS), slice(j * BS, (j + 1) * BS)
            unit = eye * coef_ref[UNIT + PB * j + p]
            mc[rows, cols] = mc[rows, cols] * coef_ref[PLAIN + j] + unit

    def back(n, carry):
        k = PB - 1 - n
        kr = pl.ds(pl.multiple_of(k * BS, BS), BS)
        rest = mc[kr, :] - three(lhi[:, kr], llo[:, kr], whi[...], wlo[...], ((0,), (0,)))
        split(whi, wlo, (kr, slice(None)), contract(dinv[k], rest, ((0,), (0,))))
        return carry

    lax.fori_loop(0, PB, back, 0)
    forward(1, 3)()

    def put(turn_at, tile):
        return pltpu.make_async_copy(
            stage_out.at[turn_at], u_ref.at[pl.ds(pl.multiple_of(tile * FW, FW), FW), :], loc.at[turn_at]
        )

    for group in range(4):
        for n in range(2):
            arrived(lane2far(0, n, group))
            if group == 3:
                for si in range(4):
                    arrived(lane2far(1, n, si))
        xx = (x + SL[group]) & 3

        def product(m, carry, group=group, xx=xx):
            yy, zz, turn_at = m >> 1, m & 1, m & 1
            tile = yy * 8 + xx * 2 + zz
            if group > 0:
                put(turn_at, 0).wait()
            else:
                pl.when(m >= 2)(lambda: put(turn_at, 0).wait())
            for colour in range(2):
                total = jnp.zeros((TR, FW), jnp.float32)
                for part, row in enumerate((yy, 3 - yy)):
                    value = gall[colour, row, xx, zz]
                    top = value.astype(jnp.bfloat16)
                    rest = (value - top.astype(jnp.float32)).astype(jnp.bfloat16)
                    rows = slice(part * TK, (part + 1) * TK)
                    total += three(top, rest, whi[rows, :], wlo[rows, :], ((1,), (0,)))
                stage_out[turn_at, colour * TR : (colour + 1) * TR, :] = total
            put(turn_at, tile).start()
            return carry

        lax.fori_loop(0, 4, product, 0)
    for turn_at in range(2):
        put(turn_at, 0).wait()

    ALL = [(c, n) for c in range(2) for n in range(2)]
    remote(ZX, recvc, recvc, partner).wait_recv()
    for part in swap:
        part.wait_send()
    rows_in.wait_send()
    for stage in range(3):
        for part, by in RELAYS:
            relay(part, stage, by, False).wait_send()

    @pl.when(source)
    def _():
        for copy in spill:
            copy.wait_send()

    for copy in across:
        copy.wait_send()
    rows_out.wait_send()
    for c, n in ALL:
        sent(lane1far(c, n))
        for d in range(2):
            sent(lane1(c, n, d))
        for si in range(4):
            sent(lane2far(c, n, si))
            for d in range(2):
                sent(lane2(c, n, si, d))


def finish(ids, at_ref, map_ref, u_ref, own, other, *refs):
    blocks, out = refs[:-1], refs[-1]
    half, grid = ids[0], ids[1]
    i = pl.program_id(0)
    out[...] = -u_ref[...]

    tile = half * (GRID // 2) + i

    def place(group, nat):
        at = jnp.int32(0)
        for s in range(1, OWN):
            at += jnp.where(at_ref[group * OWN + s] == nat, s, 0)
        return pl.multiple_of(at * BS, BS)

    for c, ref in ((half, own), (1 - half, other)):
        for a in range(HELD):
            row_nat = map_ref[c, tile * HELD + a]
            row = place(tile, row_nat)
            for t in range(HELD):
                col_nat = map_ref[c, grid * HELD + t]
                col = place(grid, col_nat)

                @pl.when((row_nat >= PB) & (col_nat >= PB))
                def _(ref=ref, a=a, t=t, row=row, col=col):
                    where = (pl.ds(row, BS), pl.ds(col, BS))
                    out[where] += ref[a * BS : (a + 1) * BS, t * BS : (t + 1) * BS]

    for s in range(OWN):
        f = at_ref[tile * OWN + s]

        @pl.when(f < PB)
        def _(s=s):
            for j in range(OWN):
                pivot = at_ref[grid * OWN + j] < PB
                out[s * BS : (s + 1) * BS, j * BS : (j + 1) * BS] = jnp.where(pivot, blocks[s * OWN + j][...], 0.0)


def factor_at(s, j):
    def index(i, ids, at_ref, map_ref):
        row = at_ref[(ids[0] * (GRID // 2) + i) * OWN + s]
        col = at_ref[ids[1] * OWN + j]
        used = (row < PB) & (col < PB)
        return jnp.where(used, row, 0), jnp.where(used, col, 0)

    return pl.BlockSpec((BS, BS), index)


def body(child_blocks, child_map, block_at, pattern):
    f32 = jnp.float32
    vmem = pl.BlockSpec(memory_space=pltpu.VMEM)
    smem = pl.BlockSpec(memory_space=pltpu.SMEM)
    hbm = pl.BlockSpec(memory_space=pltpu.HBM)
    x, xp, source, coef = pl.pallas_call(
        pick_rows,
        name="pick_rows",
        out_shape=(
            jax.ShapeDtypeStruct((PV, CW), f32),
            jax.ShapeDtypeStruct((PEERS, 16, CW), f32),
            jax.ShapeDtypeStruct((2 * PB,), jnp.int32),
            jax.ShapeDtypeStruct((COEFS,), f32),
        ),
        in_specs=[smem, smem, smem, hbm],
        out_specs=(vmem, vmem, smem, smem),
        scratch_shapes=[pltpu.SMEM((2 * PB,), jnp.int32), pltpu.SemaphoreType.DMA((PB,))],
    )(child_map, block_at, pattern, child_blocks)

    u, recvc, low = pl.pallas_call(
        exchange,
        name="exchange",
        out_shape=(
            jax.ShapeDtypeStruct((NB // 2 * BS, FW), f32),
            jax.ShapeDtypeStruct((CB // 2 * BS, CW), f32),
            jax.ShapeDtypeStruct((PV, PV), f32),
        ),
        in_specs=[smem, smem, vmem, vmem, hbm],
        out_specs=(hbm, hbm, vmem),
        scratch_shapes=[
            pltpu.VMEM((2, 4, 4, 2, TR, TK), f32),
            pltpu.VMEM((PV, CW), f32),
            pltpu.VMEM((PEERS, 16, CW), f32),
            pltpu.VMEM((3, 8, TRI // 3), f32),
            pltpu.VMEM((3, PEERS, 8, TRI // 3), f32),
            pltpu.VMEM((PV, FW), f32),
            pltpu.VMEM((2, TR, TK), f32),
            pltpu.VMEM((PV, PV), f32),
            pltpu.VMEM((PB, BS, BS), f32),
            pltpu.VMEM((BS, 2 * BS), f32),
            pltpu.VMEM((BS, 2 * BS), f32),
            pltpu.VMEM((PV, BS), f32),
            *[pltpu.VMEM((PV, PV), jnp.bfloat16)] * 2,
            *[pltpu.VMEM((PV, FW), jnp.bfloat16)] * 4,
            pltpu.VMEM((2, FW, FW), f32),
            pltpu.SemaphoreType.DMA((67,)),
            pltpu.SemaphoreType.DMA((67,)),
            pltpu.SemaphoreType.DMA((27,)),
            pltpu.SemaphoreType.DMA((27,)),
            pltpu.SemaphoreType.DMA((1,)),
            pltpu.SemaphoreType.DMA((1,)),
            pltpu.SemaphoreType.DMA((2,)),
        ],
        compiler_params=pltpu.CompilerParams(
            has_side_effects=True, collective_id=0, vmem_limit_bytes=60 * MIB
        ),
    )(source, coef, x, xp, child_blocks)

    ids = jnp.stack([lax.axis_index("half"), lax.axis_index("grid")]).astype(jnp.int32)
    return pl.pallas_call(
        finish,
        name="finish",
        out_shape=jax.ShapeDtypeStruct((NB // 2 * BS, FW), f32),
        grid_spec=pltpu.PrefetchScalarGridSpec(
            num_scalar_prefetch=3,
            grid=(GRID // 2,),
            in_specs=[
                pl.BlockSpec((FW, FW), lambda i, *_: (i, 0)),
                pl.BlockSpec((None, CW, CW), lambda i, ids, *_: (0, ids[0] * (GRID // 2) + i, 0)),
                pl.BlockSpec((CW, CW), lambda i, *_: (i, 0)),
                *[factor_at(s, j) for s in range(OWN) for j in range(OWN)],
            ],
            out_specs=pl.BlockSpec((FW, FW), lambda i, *_: (i, 0)),
        ),
        compiler_params=pltpu.CompilerParams(vmem_limit_bytes=60 * MIB),
    )(ids, block_at, child_map, u, child_blocks, recvc, *[low] * OWN**2)


def solution(mesh):
    return jax.shard_map(
        body,
        mesh=mesh,
        in_specs=(P(("cube", "half"), None, "grid"), P("cube", None), P("cube"), P("cube", None)),
        out_specs=P(("cube", "half"), "grid"),
        check_vma=False,
    )
```

```python
import jax
import jax.numpy as jnp
from jax import lax
from jax.experimental import pallas as pl
from jax.experimental.pallas import tpu as pltpu
from jax.sharding import PartitionSpec as P

BS = 128
PB = 8
PV = PB * BS
OWN = 3
HELD = 2
CW = HELD * BS
FW = OWN * BS
GRID = 32
PEERS = 2 * GRID
CB = 64
NB = 96
TR = FW // 2
TK = PV // 2
TRI = (PB + 1) * BS
MESH = pl.DeviceIdType.MESH
HI = lax.Precision.HIGHEST
MIB = 1 << 20


def contract(a, b, dims):
    return lax.dot_general(
        a, b, (dims, ((), ())), precision=HI, preferred_element_type=jnp.float32
    )


SECOND, COLUMN, KEEP, PLAIN, UNIT, COEFS = 0, 16, 28, 52, 55, 80


def pick_rows(map_ref, at_ref, pat_ref, child_ref, x_ref, xp_ref, from_ref, coef_ref, found, sems):
    half = lax.axis_index("half")
    grid = lax.axis_index("grid")

    def scan(b, carry):
        for c in range(2):
            f = map_ref[c, b]

            @pl.when(f < PB)
            def _():
                found[c * PB + f] = b

        return carry

    lax.fori_loop(0, CB, scan, 0)

    def copy(p):
        b = found[half * PB + p]
        return pltpu.make_async_copy(
            child_ref.at[0, pl.ds(pl.multiple_of(b * BS, BS), BS), :],
            x_ref.at[pl.ds(p * BS, BS), :],
            sems.at[p],
        )

    for p in range(PB):
        copy(p).start()
    for c in range(2):
        for p in range(PB):
            b = found[c * PB + p]
            from_ref[c * PB + p] = c * GRID + (b >> 1)
            coef_ref[SECOND + c * PB + p] = (b & 1).astype(jnp.float32)
    for j in range(OWN):
        q = at_ref[grid * OWN + j]
        for t in range(HELD):
            for side in range(2):
                hit = map_ref[jnp.where(side == 0, half, 1 - half), grid * HELD + t] == q
                coef_ref[COLUMN + 4 * j + 2 * t + side] = jnp.where(hit, 1.0, 0.0)
        for p in range(PB):
            keep = jnp.where(q < PB, 1, pat_ref[jnp.maximum(q - PB, 0), p])
            coef_ref[KEEP + PB * j + p] = keep.astype(jnp.float32)
            coef_ref[UNIT + PB * j + p] = jnp.where(q == p, -1.0, 0.0)
        coef_ref[PLAIN + j] = jnp.where(q < PB, 0.0, 1.0)
    for p in range(PB):
        copy(p).wait()
    for d in range(PEERS):
        xp_ref[d, 0:8, :] = x_ref[8 * d : 8 * d + 8, :]
        xp_ref[d, 8:16, :] = x_ref[PV - 8 * d - 8 : PV - 8 * d, :]


def factor_block(dy, out):
    step_rows = 16
    sub = lax.broadcasted_iota(jnp.int32, (step_rows, BS), 0)
    lane = lax.broadcasted_iota(jnp.int32, (step_rows, BS), 1)
    for j0 in range(0, BS, step_rows):
        end = j0 + step_rows
        ra = dy[j0:end, 0:BS]
        ry = dy[j0:end, BS : 2 * BS]
        cols = [
            jnp.broadcast_to(ra[:, j0 + r : j0 + r + 1], (step_rows, BS)) for r in range(step_rows)
        ]
        scale = jnp.ones((step_rows, BS), jnp.float32)
        for r in range(step_rows):
            inv = lax.rsqrt(cols[r][r : r + 1, :])
            scale = jnp.where(sub == r, inv, scale)
            if r == step_rows - 1:
                break
            part = jnp.where(sub > r, cols[r] * (inv * inv), 0.0)
            for c in range(r + 1, step_rows):
                cols[c] = cols[c] - part * cols[c][r : r + 1, :]
            ra = ra - part * ra[r : r + 1, :]
            ry = ry - part * ry[r : r + 1, :]
        ra = jnp.where(lane >= sub + j0, ra * scale, 0.0)
        both = jnp.concatenate([ra, ry * scale], axis=1)
        out[j0:end, :] = both
        if end < BS:
            top = both.astype(jnp.bfloat16)
            rest = (both - top.astype(jnp.float32)).astype(jnp.bfloat16)
            left = jnp.concatenate([top[:, 0:BS], top[:, 0:BS], rest[:, 0:BS]], axis=0)
            right = jnp.concatenate([top, rest, top], axis=0)
            step = lax.dot_general(
                left, right, (((0,), (0,)), ((), ())), preferred_element_type=jnp.float32
            )
            dy[end:, :] = dy[end:, :] - step[end:, :]


def exchange(
    from_ref, coef_ref, x_ref, xp_ref, child_ref,
    u_ref, recvc, l_out,
    l_ref, gall, xo, ra, pk, rp, mc, gt, pm, dinv, dy, uy, tcol,
    lhi, llo, vhi, vlo, whi, wlo, stage_out,
    ss, rs, bs, br, psend, precv, loc,
):
    cube = lax.axis_index("cube")
    half = lax.axis_index("half")
    grid = lax.axis_index("grid")
    me = half * GRID + grid
    y, x, zl = grid >> 3, (grid >> 1) & 3, grid & 1
    r = (y - 2 * half) & 3

    def dev(yy, xx, zz):
        return (cube, half, (yy & 3) * 8 + (xx & 3) * 2 + zz)

    partner = (cube, 1 - half, grid)

    def remote(k, src, dst, to):
        return pltpu.make_async_remote_copy(
            src_ref=src, dst_ref=dst, send_sem=ss.at[k], recv_sem=rs.at[k],
            device_id=to, device_id_type=MESH,
        )

    S0, S1, ZX, XS = (60, 61), (62, 63), 64, (65, 66)
    z = half * 2 + zl

    def at(yy, xx, zz):
        return (cube, (zz & 3) >> 1, (yy & 3) * 8 + (xx & 3) * 2 + (zz & 1))

    barrier = pltpu.get_barrier_semaphore()

    def greet(i, carry):
        to = (me + i) & (PEERS - 1)
        pl.semaphore_signal(
            barrier, inc=1, device_id=(cube, to >> 5, to & (GRID - 1)), device_id_type=MESH
        )
        return carry

    lax.fori_loop(1, PEERS, greet, 0)
    for ref in (l_ref, lhi, llo, vhi, vlo, whi, wlo):
        ref[...] = jnp.zeros_like(ref)
    pl.semaphore_wait(barrier, PEERS - 1)

    PARTS = (pl.ds(0, TK), pl.ds(TK, TK))
    swap = [remote(XS[kh], x_ref.at[PARTS[kh]], xo.at[PARTS[kh]], partner) for kh in range(2)]
    swap[1].start()
    swap[0].start()

    def spread_rows(i, carry):
        to = (me + i) & (PEERS - 1)
        pltpu.make_async_remote_copy(
            src_ref=xp_ref.at[to], dst_ref=ra.at[me], send_sem=psend.at[0], recv_sem=precv.at[0],
            device_id=(cube, to >> 5, to & (GRID - 1)), device_id_type=MESH,
        ).start()
        return carry

    lax.fori_loop(1, PEERS, spread_rows, 0)
    ra[me] = xp_ref[me]
    rows_in = pltpu.make_async_remote_copy(
        src_ref=xp_ref.at[pl.ds(0, PEERS - 1)], dst_ref=ra.at[pl.ds(0, PEERS - 1)],
        send_sem=psend.at[0], recv_sem=precv.at[0], device_id=partner, device_id_type=MESH,
    )
    rows_in.wait_recv()

    first = (me >> 4) + 1
    for k in range(PB + 1):
        low = k < first
        p = jnp.where(low, k, k - first)
        total = jnp.zeros((8, BS), jnp.float32)
        for c in range(2):
            came = ra[from_ref[c * PB + p]]
            second = coef_ref[SECOND + c * PB + p]
            came = jnp.where(low, came[0:8, :], came[8:16, :])
            total = total + came[:, 0:BS] * (1.0 - second) + came[:, BS:] * second
        pk[k // 3, :, k % 3 * BS : (k % 3 + 1) * BS] = total

    here = (z, x, y)
    ORDER = ((0, 1, 2), (1, 2, 0), (2, 0, 1))

    def bundle(part, stage, coords):
        d0, d1, d2 = ORDER[part]
        if stage == 0:
            return rp.at[part, pl.ds(coords[d2] * 16 + coords[d1] * 4 + coords[d0], 1)]
        if stage == 1:
            return rp.at[part, pl.ds(coords[d2] * 16 + coords[d1] * 4, 4)]
        return rp.at[part, pl.ds(coords[d2] * 16, 16)]

    def moved(axis, by):
        return tuple((c + by) & 3 if n == axis else c for n, c in enumerate(here))

    def relay(part, stage, by, arriving):
        axis = ORDER[part][stage]
        k = (stage * 3 + part) * 3 + by - 1
        to = moved(axis, by)
        region = bundle(part, stage, moved(axis, -by) if arriving else here)
        return pltpu.make_async_remote_copy(
            src_ref=region, dst_ref=region, send_sem=bs.at[k], recv_sem=br.at[k],
            device_id=at(to[2], to[1], to[0]), device_id_type=MESH,
        )

    RELAYS = [(part, by) for part in range(3) for by in range(1, 4)]

    def relay_start(stage):
        for part, by in RELAYS:
            relay(part, stage, by, False).start()

    def relay_wait(stage):
        for part, by in RELAYS:
            relay(part, stage, by, True).wait_recv()

    for part in range(3):
        d0, d1, d2 = ORDER[part]
        rp[part, here[d2] * 16 + here[d1] * 4 + here[d0]] = pk[part]
    relay_start(0)

    source = r < 2

    def assemble_part(kh):
        swap[kh].wait_recv()
        for j in range(OWN):

            def assemble(p, carry, j=j):
                rows = pl.ds(pl.multiple_of(p * BS, BS), BS)
                keep = coef_ref[KEEP + PB * j + p]
                total = jnp.zeros((BS, BS), jnp.float32)
                for t in range(HELD):
                    cols = slice(t * BS, (t + 1) * BS)
                    total += x_ref[rows, cols] * coef_ref[COLUMN + 4 * j + 2 * t]
                    total += xo[rows, cols] * coef_ref[COLUMN + 4 * j + 2 * t + 1]
                mc[rows, j * BS : (j + 1) * BS] = total * keep
                return carry

            lax.fori_loop(kh * PB // 2, (kh + 1) * PB // 2, assemble, 0)

    def slot(c, a, b, n):
        level = zl if n == 0 else 1 - zl
        return gall.at[0, b & 3, a & 3, level] if c == 0 else gall.at[1, a & 3, b & 3, level]

    mya, myb = (x, r), (r, x)
    turn = (zl, 1 - zl)

    def toward(c, dim, delta):
        along_x = (c == 0) == (dim == 1)
        return dev(y, x + delta, zl) if along_x else dev(y + delta, x, zl)

    SL = (0, -1, 1, 2)

    def lane1(c, n, d):
        step = 1 - 2 * d
        s = slot(c, mya[c], myb[c], n)
        return s, slot(c, mya[c] - step, myb[c], n), toward(c, 1, step), c * 30 + n * 15 + d

    def lane1far(c, n):
        step = 1 - 2 * turn[n]
        a, b = mya[c], myb[c]
        return slot(c, a - step, b, n), slot(c, a - 2 * step, b, n), toward(c, 1, step), c * 30 + n * 15 + 2

    def lane2(c, n, si, d):
        step = 1 - 2 * d
        a, b = mya[c] + SL[si], myb[c]
        k = c * 30 + n * 15 + 3 + si * 3 + d
        return slot(c, a, b, n), slot(c, a, b - step, n), toward(c, 2, step), k

    def lane2far(c, n, si):
        step = 1 - 2 * turn[n]
        a, b = mya[c] + SL[si], myb[c]
        k = c * 30 + n * 15 + 3 + si * 3 + 2
        return slot(c, a, b - step, n), slot(c, a, b - 2 * step, n), toward(c, 2, step), k

    def start(lane):
        remote(lane[3], lane[0], lane[0], lane[2]).start()

    def arrived(lane):
        remote(lane[3], lane[1], lane[1], partner).wait_recv()

    def sent(lane):
        remote(lane[3], lane[0], lane[0], lane[2]).wait_send()

    def own_ready(n, c):
        for d in range(2):
            start(lane1(c, n, d))
            start(lane2(c, n, 0, d))

    def near(n):
        def run():
            for d in range(2):
                for c in range(2):
                    arrived(lane1(c, n, d))
                    for e in range(2):
                        start(lane2(c, n, 1 + d, e))
            for c in range(2):
                start(lane1far(c, n))

        return run

    def far(n):
        def run():
            for c in range(2):
                arrived(lane1far(c, n))
                for d in range(2):
                    start(lane2(c, n, 3, d))

        return run

    def forward(n, si):
        def run():
            for c in range(2):
                for d in range(2):
                    arrived(lane2(c, n, si, d))
                start(lane2far(c, n, si))

        return run

    shard = [gall.at[c, r, x, zl] for c in range(2)]
    spill = [
        remote(S0[c], gt.at[c], gall.at[c, (3 - r) & 3, x, zl], dev(jnp.where(r == 0, y - 1, y + 1), x, zl))
        for c in range(2)
    ]
    across = [remote(S1[c], shard[c], shard[c], dev(y, x, 1 - zl)) for c in range(2)]

    assemble_part(1)

    @pl.when(source)
    def _():
        piece = mc[TK:PV, :].T
        for c in range(2):
            gt[c] = piece[c * TR : (c + 1) * TR, :]
            spill[c].start()

    relay_wait(0)
    relay_start(1)
    assemble_part(0)

    @pl.when(source)
    def _():
        piece = mc[0:TK, :].T
        for c in range(2):
            gall[c, r, x, zl] = piece[c * TR : (c + 1) * TR, :]
            across[c].start()
            own_ready(0, c)

    relay_wait(1)
    relay_start(2)

    @pl.when(jnp.logical_not(source))
    def _():
        for c in range(2):
            remote(S0[c], gt.at[c], shard[c], partner).wait_recv()
            across[c].start()
            own_ready(0, c)

    rows_out = remote(
        ZX,
        child_ref.at[0, pl.ds(pl.multiple_of((1 - half) * (CB // 2 * BS), BS), CB // 2 * BS), :],
        recvc,
        partner,
    )

    def other_ready():
        for c in range(2):
            remote(S1[c], shard[c], gall.at[c, r, x, 1 - zl], partner).wait_recv()
            own_ready(1, c)

    events = {
        (0, 0): [near(0)],
        (1, 0): [forward(0, 0), rows_out.start],
        (1, 1): [near(1)],
        (2, 1): [forward(1, 0)],
        (3, 1): [far(0)],
        (4, 0): [forward(0, 1)],
        (4, 1): [forward(0, 2)],
        (5, 0): [far(1)],
        (5, 1): [forward(1, 1)],
        (6, 0): [forward(1, 2)],
        (7, 0): [forward(0, 3)],
    }

    def follow(k, part):
        for (step, at_part), todo in events.items():
            if at_part == part:

                @pl.when(k == step)
                def _(todo=todo):
                    for event in todo:
                        event()

    relay_wait(2)
    other_ready()
    for group in range(4):
        w1 = group + 1

        def unpack(i, carry, group=group, w1=w1):
            yy, xx, zz = (group & 1) * 2 + (i >> 3), (i >> 1) & 3, (group >> 1) * 2 + (i & 1)
            d = group * 16 + i
            lo = pl.ds(pl.multiple_of(8 * d, 8), 8)
            hi = pl.ds(pl.multiple_of(PV - 8 - 8 * d, 8), 8)
            index = (yy * 16 + xx * 4 + zz, zz * 16 + yy * 4 + xx, xx * 16 + zz * 4 + yy)
            for k in range(PB + 1):
                share = rp[k // 3, index[k // 3], :, k % 3 * BS : (k % 3 + 1) * BS]
                if k < w1:
                    pm[lo, k * BS : (k + 1) * BS] = share
                else:
                    pm[hi, (k - w1) * BS : (k - w1 + 1) * BS] = share
            return carry

        lax.fori_loop(0, 16, unpack, 0)

    rowi = lax.broadcasted_iota(jnp.int32, (BS, BS), 0)
    coli = lax.broadcasted_iota(jnp.int32, (BS, BS), 1)
    eye = (rowi == coli).astype(jnp.float32)

    def split(ref_hi, ref_lo, where, value):
        top = value.astype(jnp.bfloat16)
        ref_hi[where] = top
        ref_lo[where] = (value - top.astype(jnp.float32)).astype(jnp.bfloat16)

    def three(ahi, alo, bhi, blo, dims):
        def dot(a, b):
            return lax.dot_general(a, b, (dims, ((), ())), preferred_element_type=jnp.float32)

        return dot(ahi, bhi) + dot(ahi, blo) + dot(alo, bhi)

    def panel(k, carry):
        kk = pl.multiple_of(k * BS, BS)
        kr = pl.ds(kk, BS)

        def reduce_by(known):
            def trail(i, c):
                ir = pl.ds(pl.multiple_of(i * BS, BS), BS)
                tcol[ir, :] = pm[ir, kr] - three(
                    lhi[ir, 0:known], llo[ir, 0:known], lhi[kr, 0:known], llo[kr, 0:known], ((1,), (1,))
                )
                return c

            lax.fori_loop(k, PB, trail, 0)
            mc[kr, :] = mc[kr, :] - three(
                lhi[kr, 0:known], llo[kr, 0:known], vhi[0:known, :], vlo[0:known, :], ((1,), (0,))
            )

        pl.when(k < PB // 2)(lambda: reduce_by(TK))
        pl.when(k >= PB // 2)(lambda: reduce_by(PV))

        follow(k, 0)
        dy[:, 0:BS] = tcol[kr, :]
        dy[:, BS:] = eye
        factor_block(dy, uy)
        inv = uy[:, BS:]
        solved = contract(inv, mc[kr, :], ((1,), (0,)))
        mc[kr, :] = solved
        split(vhi, vlo, (kr, slice(None)), solved)
        dinv[k] = inv
        l_ref[kr, kr] = uy[:, 0:BS].T

        def below(i, c):
            ir = pl.ds(pl.multiple_of(i * BS, BS), BS)
            got = contract(tcol[ir, :], inv, ((1,), (1,)))
            l_ref[ir, kr] = got
            split(lhi, llo, (ir, kr), got)
            return c

        lax.fori_loop(k + 1, PB, below, 0)
        follow(k, 1)
        return carry

    lax.fori_loop(0, PB, panel, 0)
    factor_out = pltpu.make_async_copy(l_ref, l_out, loc.at[2])
    factor_out.start()

    for j in range(OWN):
        for p in range(PB):
            rows, cols = slice(p * BS, (p + 1) * BS), slice(j * BS, (j + 1) * BS)
            unit = eye * coef_ref[UNIT + PB * j + p]
            mc[rows, cols] = mc[rows, cols] * coef_ref[PLAIN + j] + unit

    def back(n, carry):
        k = PB - 1 - n
        kr = pl.ds(pl.multiple_of(k * BS, BS), BS)
        rest = mc[kr, :] - three(lhi[:, kr], llo[:, kr], whi[...], wlo[...], ((0,), (0,)))
        split(whi, wlo, (kr, slice(None)), contract(dinv[k], rest, ((0,), (0,))))
        return carry

    lax.fori_loop(0, PB, back, 0)
    forward(1, 3)()

    def put(turn_at, tile):
        return pltpu.make_async_copy(
            stage_out.at[turn_at], u_ref.at[pl.ds(pl.multiple_of(tile * FW, FW), FW), :], loc.at[turn_at]
        )

    for done, (group, n) in enumerate([(0, 0), (1, 0), (2, 0), (0, 1), (1, 1), (2, 1), (3, 0), (3, 1)]):
        arrived(lane2far(0, n, group))
        if group == 3:
            for si in range(4):
                arrived(lane2far(1, n, si))
        xx = (x + SL[group]) & 3
        level = zl if n == 0 else 1 - zl

        def product(yy, carry, done=done, xx=xx, level=level):
            tile = yy * 8 + xx * 2 + level
            if done > 0:
                put(yy, 0).wait()
            for colour in range(2):
                total = jnp.zeros((TR, FW), jnp.float32)
                for part, row in enumerate((yy, 3 - yy)):
                    value = gall[colour, row, xx, level]
                    top = value.astype(jnp.bfloat16)
                    rest = (value - top.astype(jnp.float32)).astype(jnp.bfloat16)
                    rows = slice(part * TK, (part + 1) * TK)
                    total += three(top, rest, whi[rows, :], wlo[rows, :], ((1,), (0,)))
                stage_out[yy, colour * TR : (colour + 1) * TR, :] = total
            put(yy, tile).start()
            return carry

        lax.fori_loop(0, 2, product, 0)
    for turn_at in range(2):
        put(turn_at, 0).wait()
    factor_out.wait()

    ALL = [(c, n) for c in range(2) for n in range(2)]
    remote(ZX, recvc, recvc, partner).wait_recv()
    for part in swap:
        part.wait_send()
    rows_in.wait_send()
    for stage in range(3):
        for part, by in RELAYS:
            relay(part, stage, by, False).wait_send()

    @pl.when(source)
    def _():
        for copy in spill:
            copy.wait_send()

    for copy in across:
        copy.wait_send()
    rows_out.wait_send()
    for c, n in ALL:
        sent(lane1far(c, n))
        for d in range(2):
            sent(lane1(c, n, d))
        for si in range(4):
            sent(lane2far(c, n, si))
            for d in range(2):
                sent(lane2(c, n, si, d))


def finish(ids, at_ref, map_ref, u_ref, own, other, *refs):
    blocks, out = refs[:-1], refs[-1]
    half, grid = ids[0], ids[1]
    i = pl.program_id(0)
    out[...] = -u_ref[...]

    tile = half * (GRID // 2) + i

    def place(group, nat):
        at = jnp.int32(0)
        for s in range(1, OWN):
            at += jnp.where(at_ref[group * OWN + s] == nat, s, 0)
        return pl.multiple_of(at * BS, BS)

    for c, ref in ((half, own), (1 - half, other)):
        for a in range(HELD):
            row_nat = map_ref[c, tile * HELD + a]
            row = place(tile, row_nat)
            for t in range(HELD):
                col_nat = map_ref[c, grid * HELD + t]
                col = place(grid, col_nat)

                @pl.when((row_nat >= PB) & (col_nat >= PB))
                def _(ref=ref, a=a, t=t, row=row, col=col):
                    where = (pl.ds(row, BS), pl.ds(col, BS))
                    out[where] += ref[a * BS : (a + 1) * BS, t * BS : (t + 1) * BS]

    for s in range(OWN):
        f = at_ref[tile * OWN + s]

        @pl.when(f < PB)
        def _(s=s):
            for j in range(OWN):
                pivot = at_ref[grid * OWN + j] < PB
                out[s * BS : (s + 1) * BS, j * BS : (j + 1) * BS] = jnp.where(pivot, blocks[s * OWN + j][...], 0.0)


def factor_at(s, j):
    def index(i, ids, at_ref, map_ref):
        row = at_ref[(ids[0] * (GRID // 2) + i) * OWN + s]
        col = at_ref[ids[1] * OWN + j]
        used = (row < PB) & (col < PB)
        return jnp.where(used, row, 0), jnp.where(used, col, 0)

    return pl.BlockSpec((BS, BS), index)


def body(child_blocks, child_map, block_at, pattern):
    f32 = jnp.float32
    vmem = pl.BlockSpec(memory_space=pltpu.VMEM)
    smem = pl.BlockSpec(memory_space=pltpu.SMEM)
    hbm = pl.BlockSpec(memory_space=pltpu.HBM)
    x, xp, source, coef = pl.pallas_call(
        pick_rows,
        name="pick_rows",
        out_shape=(
            jax.ShapeDtypeStruct((PV, CW), f32),
            jax.ShapeDtypeStruct((PEERS, 16, CW), f32),
            jax.ShapeDtypeStruct((2 * PB,), jnp.int32),
            jax.ShapeDtypeStruct((COEFS,), f32),
        ),
        in_specs=[smem, smem, smem, hbm],
        out_specs=(vmem, vmem, smem, smem),
        scratch_shapes=[pltpu.SMEM((2 * PB,), jnp.int32), pltpu.SemaphoreType.DMA((PB,))],
    )(child_map, block_at, pattern, child_blocks)

    u, recvc, low = pl.pallas_call(
        exchange,
        name="exchange",
        out_shape=(
            jax.ShapeDtypeStruct((NB // 2 * BS, FW), f32),
            jax.ShapeDtypeStruct((CB // 2 * BS, CW), f32),
            jax.ShapeDtypeStruct((PV, PV), f32),
        ),
        in_specs=[smem, smem, vmem, vmem, hbm],
        out_specs=(hbm, hbm, hbm),
        scratch_shapes=[
            pltpu.VMEM((PV, PV), f32),
            pltpu.VMEM((2, 4, 4, 2, TR, TK), f32),
            pltpu.VMEM((PV, CW), f32),
            pltpu.VMEM((PEERS, 16, CW), f32),
            pltpu.VMEM((3, 8, TRI // 3), f32),
            pltpu.VMEM((3, PEERS, 8, TRI // 3), f32),
            pltpu.VMEM((PV, FW), f32),
            pltpu.VMEM((2, TR, TK), f32),
            pltpu.VMEM((PV, PV), f32),
            pltpu.VMEM((PB, BS, BS), f32),
            pltpu.VMEM((BS, 2 * BS), f32),
            pltpu.VMEM((BS, 2 * BS), f32),
            pltpu.VMEM((PV, BS), f32),
            *[pltpu.VMEM((PV, PV), jnp.bfloat16)] * 2,
            *[pltpu.VMEM((PV, FW), jnp.bfloat16)] * 4,
            pltpu.VMEM((2, FW, FW), f32),
            pltpu.SemaphoreType.DMA((67,)),
            pltpu.SemaphoreType.DMA((67,)),
            pltpu.SemaphoreType.DMA((27,)),
            pltpu.SemaphoreType.DMA((27,)),
            pltpu.SemaphoreType.DMA((1,)),
            pltpu.SemaphoreType.DMA((1,)),
            pltpu.SemaphoreType.DMA((3,)),
        ],
        compiler_params=pltpu.CompilerParams(
            has_side_effects=True, collective_id=0, vmem_limit_bytes=60 * MIB
        ),
    )(source, coef, x, xp, child_blocks)

    ids = jnp.stack([lax.axis_index("half"), lax.axis_index("grid")]).astype(jnp.int32)
    return pl.pallas_call(
        finish,
        name="finish",
        out_shape=jax.ShapeDtypeStruct((NB // 2 * BS, FW), f32),
        grid_spec=pltpu.PrefetchScalarGridSpec(
            num_scalar_prefetch=3,
            grid=(GRID // 2,),
            in_specs=[
                pl.BlockSpec((FW, FW), lambda i, *_: (i, 0)),
                pl.BlockSpec((None, CW, CW), lambda i, ids, *_: (0, ids[0] * (GRID // 2) + i, 0)),
                pl.BlockSpec((CW, CW), lambda i, *_: (i, 0)),
                *[factor_at(s, j) for s in range(OWN) for j in range(OWN)],
            ],
            out_specs=pl.BlockSpec((FW, FW), lambda i, *_: (i, 0)),
        ),
        compiler_params=pltpu.CompilerParams(vmem_limit_bytes=60 * MIB),
    )(ids, block_at, child_map, u, child_blocks, recvc, *[low] * OWN**2)


def solution(mesh):
    return jax.shard_map(
        body,
        mesh=mesh,
        in_specs=(P(("cube", "half"), None, "grid"), P("cube", None), P("cube"), P("cube", None)),
        out_specs=P(("cube", "half"), "grid"),
        check_vma=False,
    )
```
